32 devices in a mesh: grp: 2 (over y), lib: 4 (over x, core), ptl: 4 (over z).
Axes of the slice: x: 2, y: 2, z: 4, core: 2. Of those that a mesh axis runs over, the one named last changes fastest.
Arguments:
- particles: bfloat16 [1536, 9984], P(('grp', 'lib', 'ptl')), parts along dimension 0
- shifts: int32 [1536], P(('grp', 'lib', 'ptl')), parts along dimension 0, may hold values from 0 to 8
- references: bfloat16 [1024, 9984], P(('grp', 'lib')), parts along dimension 0
- inv_noise: float32 [9984], P('grp'), parts along dimension 0, may hold values from 0.015024038 to 0.060096152
- proj_class: int32 [512], P('lib'), may hold values from 0 to 15
Outputs:
- log_evidence: float32 [1536], P(('grp', 'lib', 'ptl')), parts along dimension 0
- class_posterior: float32 [1536, 16], P(('grp', 'lib', 'ptl')), parts along dimension 0
- weighted_sums: float32 [1024, 9984], P(('grp', 'lib'), 'ptl'), parts along dimension 0
- weight_totals: float32 [1024], P(('grp', 'lib', 'ptl')), parts along dimension 0
The draws below stay inside these ranges and needn't reach their ends.
There are 2 independent parts, one for each index of `grp`. The reference program is written for one: setup_inputs(seed, part) draws one part's arguments, and reference() takes and returns one part's arrays. A program takes and returns all parts, laid end to end along the dimension named above; an argument that names none is the same for every part. Nothing has to cross between parts.
All inputs are finite; a program needn't handle non-finite values.
Results may differ from the reference program's by a relative error of at most 0.0085.
Values may be sent and summed in bfloat16 or wider, within the bound.
A program may use at most 64 MiB of HBM per device.

```python
import math
import jax
import jax.numpy as jnp
from jax import lax

K = 4992
CLASSES = 16
PART_DEV = 48
P_SIZE = 512
N = 768
N_LIB = 4
N_PTL = 4


def ref_field(key):
    signs = jax.random.rademacher(jax.random.fold_in(key, 11), (P_SIZE, 2 * K), jnp.float32)
    magnitude = jax.random.uniform(jax.random.fold_in(key, 13), (P_SIZE, 2 * K), jnp.float32, 0.85, 1.15)
    return signs * magnitude


def shift_field(key):
    return jax.random.randint(jax.random.fold_in(key, 17), (N,), 0, 9, dtype=jnp.int32)


def draw_references(key, part):
    return ref_field(key).astype(jnp.bfloat16)


def draw_shifts(key, part):
    return shift_field(key)


def draw_particles(key, part):
    target = 0.35 * jnp.clip(jax.random.normal(jax.random.fold_in(key, 23), (N, 2 * K), jnp.float32), -5.0, 5.0)
    shift_ids = shift_field(key)
    freq_index = jnp.arange(K, dtype=jnp.int32)
    freq_x = (freq_index % 64).astype(jnp.float32)
    freq_y = (freq_index // 64).astype(jnp.float32)
    step_x = (shift_ids % 3 - 1).astype(jnp.float32)
    step_y = (shift_ids // 3 - 1).astype(jnp.float32)
    angle = (step_x[:, None] * freq_x[None, :] + step_y[:, None] * freq_y[None, :]) * (2.0 * math.pi / 128.0)
    cosine = jnp.cos(angle)
    sine = jnp.sin(angle)
    real_part = target[:, :K]
    imag_part = target[:, K:]
    return jnp.concatenate([real_part * cosine - imag_part * sine, real_part * sine + imag_part * cosine], axis=1).astype(jnp.bfloat16)


def with_ends(entries, key, low, high):
    longest = entries.shape.index(max(entries.shape))
    spots = []
    for shift in (0, 1):
        where = [jax.random.randint(jax.random.fold_in(key, axis), (), 0, length) for axis, length in enumerate(entries.shape)]
        where[longest] = (where[longest] + shift) % entries.shape[longest]
        spots.append(tuple(where))
    return entries.at[spots[0]].set(low).at[spots[1]].set(high)


def setup_inputs(seed: int = 0, part: int = 0) -> dict:
    arg_keys = jax.random.split(jax.random.key(seed), 6)
    part_keys = jax.random.split(jax.random.fold_in(arg_keys[5], part), 6)
    particles = draw_particles(jax.random.fold_in(jax.random.fold_in(arg_keys[5], part), 71), part)
    shifts = draw_shifts(jax.random.fold_in(jax.random.fold_in(arg_keys[5], part), 71), part)
    references = draw_references(jax.random.fold_in(jax.random.fold_in(arg_keys[5], part), 71), part)
    inv_noise = jnp.clip(jnp.exp(jax.random.uniform(part_keys[3], (K,), jnp.float32, math.log(0.015024038), math.log(0.060096152))), 0.015024038, 0.060096152)
    proj_class = with_ends(jax.random.randint(arg_keys[4], (P_SIZE,), 0, CLASSES), jax.random.fold_in(arg_keys[4], 1), 0, CLASSES - 1).astype(jnp.int32)
    return {"particles": particles, "shifts": shifts, "references": references, "inv_noise": inv_noise, "proj_class": proj_class}


def shift_images(images, shift_ids):
    half_width = images.shape[1] // 2
    freq_index = jnp.arange(half_width, dtype=jnp.int32)
    freq_x = (freq_index % 64).astype(jnp.float32)
    freq_y = (freq_index // 64).astype(jnp.float32)
    step_x = (shift_ids % 3 - 1).astype(jnp.float32)
    step_y = (shift_ids // 3 - 1).astype(jnp.float32)
    angle = (step_x[:, None] * freq_x[None, :] + step_y[:, None] * freq_y[None, :]) * (2.0 * math.pi / 128.0)
    cosine = jnp.cos(angle)
    sine = jnp.sin(angle)
    real_part = images[:, :half_width].astype(jnp.float32)
    imag_part = images[:, half_width:].astype(jnp.float32)
    return jnp.concatenate([real_part * cosine + imag_part * sine, imag_part * cosine - real_part * sine], axis=1).astype(jnp.bfloat16)


def prepare_refs(references, inv_noise):
    doubled = jnp.concatenate([inv_noise, inv_noise])
    widened = references.astype(jnp.float32)
    weighted = (widened * doubled[None, :]).astype(jnp.bfloat16)
    half_norm = 0.5 * jnp.sum(widened * widened * doubled[None, :], axis=1)
    return weighted, half_norm


def score_rows(rows, weighted, half_norm):
    return lax.dot_general(rows, weighted, (((1,), (1,)), ((), ())), preferred_element_type=jnp.float32) - half_norm[None, :]


def reference(particles, shifts, references, inv_noise, proj_class):
    shifted = shift_images(particles, shifts)
    weighted, half_norm = prepare_refs(references, inv_noise)
    onehot = (proj_class[:, None] == jnp.arange(CLASSES, dtype=jnp.int32)[None, :]).astype(jnp.bfloat16)
    width = shifted.shape[1]
    grouped = shifted.reshape(N_LIB, N_PTL, PART_DEV, width).transpose(1, 0, 2, 3).reshape(N_PTL, N_LIB * PART_DEV, width)

    def one_group(carry, rows):
        scores = score_rows(rows, weighted, half_norm)
        peak = jnp.max(scores, axis=1)
        evidence = peak + jnp.log(jnp.sum(jnp.exp(scores - peak[:, None]), axis=1))
        post_weights = jnp.exp(scores - evidence[:, None]).astype(jnp.bfloat16)
        shares = jnp.dot(post_weights, onehot, preferred_element_type=jnp.float32)
        sums = lax.dot_general(post_weights, rows, (((0,), (0,)), ((), ())), preferred_element_type=jnp.float32)
        sums = lax.optimization_barrier(sums.astype(jnp.bfloat16)).astype(jnp.float32)
        totals = jnp.sum(post_weights.astype(jnp.float32), axis=0)
        totals = lax.optimization_barrier(totals.astype(jnp.bfloat16)).astype(jnp.float32)
        return (carry[0] + sums, carry[1] + totals), (evidence, shares)

    start = (jnp.zeros((weighted.shape[0], width), jnp.float32), jnp.zeros((weighted.shape[0],), jnp.float32))
    (sums, totals), (evidence, shares) = lax.scan(one_group, start, grouped)
    evidence = evidence.reshape(N_PTL, N_LIB, PART_DEV).transpose(1, 0, 2).reshape(-1)
    shares = shares.reshape(N_PTL, N_LIB, PART_DEV, CLASSES).transpose(1, 0, 2, 3).reshape(-1, CLASSES)
    return (evidence, shares, sums, totals)
```

```python
import functools
import math

import jax
import jax.numpy as jnp
import numpy as np
from jax import lax
from jax.experimental import pallas as pl
from jax.experimental.pallas import tpu as pltpu
from jax.sharding import PartitionSpec as P

CLASSES = 16
LANES = 128


def run_loop(low, high, body):
    if high - low <= 4:
        for index in range(low, high):
            body(index)
    else:

        def step(index, carry):
            body(index)
            return carry

        lax.fori_loop(low, high, step, 0)


def hop(index, count):
    odd = index % 2
    return odd * ((index + 1) // 2) + (1 - odd) * (count - index // 2)


def kernel(
    n_lib,
    n_ptl,
    span,
    part_ref,
    shift_ref,
    table_ref,
    refs_hbm,
    noise_ref,
    class_ref,
    sums_ref,
    evid_ref,
    share_ref,
    total_ref,
    shifted,
    gath,
    refbuf,
    weighted,
    spart,
    srecv,
    post,
    stat,
    stat_in,
    share_out,
    share_in,
    totbuf,
    ref_sem,
    own_sem,
    z_send,
    z_recv,
    x_send,
    x_recv,
    c_send,
    c_recv,
    s_send,
    s_recv,
    t_send,
    t_recv,
    p_send,
    p_recv,
    h_send,
    h_recv,
):
    lib = lax.axis_index("lib")
    ptl = lax.axis_index("ptl")
    n_x = n_lib // 2
    x, core = lib // 2, lib % 2
    mate = 2 * x + 1 - core
    rows, width = part_ref.shape
    half = width // 2
    part_cols = width // n_ptl
    tiles = width // LANES

    def first_tile(z):
        return jnp.minimum((z * part_cols) // LANES, tiles - span // LANES)

    def chunk(z):
        return pl.ds(pl.multiple_of(first_tile(z) * LANES, LANES), span)

    barrier = pltpu.get_barrier_semaphore()

    def greet_ptl(step):
        pl.semaphore_signal(barrier, inc=1, device_id={"ptl": lax.rem(ptl + step, n_ptl)})

    def greet_lib(step):
        pl.semaphore_signal(barrier, inc=1, device_id={"lib": lax.rem(lib + step, n_lib)})

    run_loop(1, n_ptl, greet_ptl)
    run_loop(1, n_lib, greet_lib)

    ref_copy = pltpu.make_async_copy(refs_hbm.at[:, chunk(ptl)], refbuf, ref_sem)
    ref_copy.start()

    ids = shift_ref[...]
    step_y = (ids >= 3).astype(jnp.int32) + (ids >= 6).astype(jnp.int32)
    step_x = (ids - 3 * step_y - 1).astype(jnp.float32)
    step_y = (step_y - 1).astype(jnp.float32)
    cos_x = jnp.where(step_x == 0.0, 1.0, table_ref[0:1, 0:LANES])
    sin_x = step_x * table_ref[1:2, 0:LANES]
    for tile in range(half // LANES):
        lo = slice(tile * LANES, (tile + 1) * LANES)
        hi = slice(half + tile * LANES, half + (tile + 1) * LANES)
        cos_y = jnp.where(step_y == 0.0, 1.0, table_ref[2:3, lo])
        sin_y = step_y * table_ref[3:4, lo]
        cosine = cos_x * cos_y - sin_x * sin_y
        sine = sin_x * cos_y + cos_x * sin_y
        real = part_ref[:, lo].astype(jnp.float32)
        imag = part_ref[:, hi].astype(jnp.float32)
        shifted[:, lo] = (real * cosine + imag * sine).astype(jnp.bfloat16)
        shifted[:, hi] = (imag * cosine - real * sine).astype(jnp.bfloat16)

    pl.semaphore_wait(barrier, n_ptl - 1 + n_lib - 1)

    def z_copy(i):
        to = lax.rem(ptl + hop(i, n_ptl), n_ptl)
        return pltpu.make_async_remote_copy(
            src_ref=shifted.at[:, chunk(to)],
            dst_ref=gath.at[i, lib],
            send_sem=z_send.at[i - 1],
            recv_sem=z_recv.at[i - 1],
            device_id={"ptl": to},
        )

    run_loop(1, n_ptl, lambda i: z_copy(i).start())
    own_copy = pltpu.make_async_copy(shifted.at[:, chunk(ptl)], gath.at[0, lib], own_sem)
    own_copy.start()

    def x_copy(i, d):
        return pltpu.make_async_remote_copy(
            src_ref=gath.at[i, lib],
            dst_ref=gath.at[i, lib],
            send_sem=x_send.at[i, d - 1],
            recv_sem=x_recv.at[i, d - 1],
            device_id={"lib": lax.rem(x + d, n_x) * 2 + core},
        )

    def x_arrival(i, d):
        source = lax.rem(x - d + n_x, n_x) * 2 + core
        return pltpu.make_async_remote_copy(
            src_ref=gath.at[i, source],
            dst_ref=gath.at[i, source],
            send_sem=x_send.at[i, d - 1],
            recv_sem=x_recv.at[i, d - 1],
            device_id={"lib": source},
        )

    def core_copy(i, d):
        source = lax.rem(x - d + n_x, n_x) * 2 + core
        return pltpu.make_async_remote_copy(
            src_ref=gath.at[i, source],
            dst_ref=gath.at[i, source],
            send_sem=c_send.at[i, d],
            recv_sem=c_recv.at[i, d],
            device_id={"lib": mate},
        )

    def core_arrival(i, d):
        source = lax.rem(x - d + n_x, n_x) * 2 + 1 - core
        return pltpu.make_async_remote_copy(
            src_ref=gath.at[i, source],
            dst_ref=gath.at[i, source],
            send_sem=c_send.at[i, d],
            recv_sem=c_recv.at[i, d],
            device_id={"lib": mate},
        )

    def z_arrival(i):
        source = lax.rem(ptl - hop(i, n_ptl) + n_ptl, n_ptl)
        return pltpu.make_async_remote_copy(
            src_ref=shifted.at[:, chunk(ptl)],
            dst_ref=gath.at[i, lib],
            send_sem=z_send.at[i - 1],
            recv_sem=z_recv.at[i - 1],
            device_id={"ptl": source},
        )

    def spread(i):
        run_loop(1, n_x, lambda d: x_copy(i, d).start())
        core_copy(i, 0).start()

    def score_copy(i):
        return pltpu.make_async_remote_copy(
            src_ref=spart.at[i],
            dst_ref=srecv.at[i - 1],
            send_sem=s_send.at[i - 1],
            recv_sem=s_recv.at[i - 1],
            device_id={"ptl": lax.rem(ptl - hop(i, n_ptl) + n_ptl, n_ptl)},
        )

    def relay(i):
        def forward(d):
            x_arrival(i, d).wait_recv()
            core_copy(i, d).start()

        run_loop(1, n_x, forward)
        run_loop(0, n_x, lambda d: core_arrival(i, d).wait_recv())

    def score(i):
        block = gath[i].reshape(n_lib * rows, span)
        spart[i] = (
            lax.dot_general(
                weighted[...], block, (((1,), (1,)), ((), ())), preferred_element_type=jnp.float32
            )
            - half_norm
        )

    own_copy.wait()
    spread(0)

    ref_copy.wait()
    offset = ptl * part_cols - first_tile(ptl) * LANES
    place = lax.broadcasted_iota(jnp.int32, (1, span), 1)
    inside = (place >= offset) & (place < offset + part_cols)
    noise = jnp.where(inside, noise_ref[:, chunk(ptl)], 0.0)
    widened = refbuf[...].astype(jnp.float32)
    scaled = widened * noise
    weighted[...] = scaled.astype(jnp.bfloat16)
    half_norm = 0.5 * jnp.sum(widened * scaled, axis=1, keepdims=True)

    def advance(i):
        z_arrival(i).wait_recv()
        spread(i)
        relay(i - 1)
        score(i - 1)

    z_arrival(1).wait_recv()
    spread(1)
    relay(0)
    score(0)

    def middle(i):
        advance(i)
        score_copy(i - 1).start()

    run_loop(2, n_ptl, middle)
    relay(n_ptl - 1)
    score(n_ptl - 1)
    score_copy(n_ptl - 1).start()

    def add_scores(i):
        score_copy(i).wait_recv()
        spart[0] = spart[0] + srecv[i - 1]

    run_loop(1, n_ptl, add_scores)
    scores = spart[0]

    peak = jnp.max(scores, axis=0, keepdims=True)
    stat[0:1] = peak
    stat[1:2] = jnp.sum(jnp.exp(scores - peak), axis=0, keepdims=True)

    def stat_copy(d):
        return pltpu.make_async_remote_copy(
            src_ref=stat,
            dst_ref=stat_in.at[d],
            send_sem=t_send.at[d - 1],
            recv_sem=t_recv.at[d - 1],
            device_id={"lib": lax.rem(lib + d, n_lib)},
        )

    run_loop(1, n_lib, lambda d: stat_copy(d).start())
    stat_in[0, 0:2] = stat[0:2]
    run_loop(1, n_lib, lambda d: stat_copy(d).wait_recv())
    top = peak
    for d in range(1, n_lib):
        top = jnp.maximum(top, stat_in[d, 0:1])
    total = jnp.zeros_like(top)
    for d in range(n_lib):
        total = total + stat_in[d, 1:2] * jnp.exp(stat_in[d, 0:1] - top)
    evidence = top + jnp.log(total)
    evid_ref[...] = evidence
    own_post = jnp.exp(scores - evidence).astype(jnp.bfloat16)
    post[0] = own_post

    def post_copy(i):
        return pltpu.make_async_remote_copy(
            src_ref=post.at[0],
            dst_ref=post.at[i],
            send_sem=p_send.at[i - 1],
            recv_sem=p_recv.at[i - 1],
            device_id={"ptl": lax.rem(ptl + hop(i, n_ptl), n_ptl)},
        )

    run_loop(1, n_ptl, lambda i: post_copy(i).start())

    onehot = (
        class_ref[...] == lax.broadcasted_iota(jnp.int32, (class_ref.shape[0], CLASSES), 1)
    ).astype(jnp.bfloat16)
    share_out[...] = lax.dot_general(
        own_post, onehot, (((0,), (0,)), ((), ())), preferred_element_type=jnp.float32
    ).reshape(n_lib, rows, CLASSES)

    def share_copy(d):
        to = lax.rem(lib + d, n_lib)
        return pltpu.make_async_remote_copy(
            src_ref=share_out.at[to],
            dst_ref=share_in.at[d - 1],
            send_sem=h_send.at[d - 1],
            recv_sem=h_recv.at[d - 1],
            device_id={"lib": to},
        )

    run_loop(1, n_lib, lambda d: share_copy(d).start())

    block = 512 if span % 512 == 0 else LANES

    def own_sums(b):
        cols = pl.ds(pl.multiple_of(b * block, block), block)
        images = gath[0, :, :, cols].reshape(n_lib * rows, block)
        sums_ref[:, cols] = jnp.dot(own_post, images, preferred_element_type=jnp.float32)

    lax.fori_loop(0, span // block, lambda b, c: (own_sums(b), c)[1], 0)

    totbuf[...] = jnp.sum(own_post.astype(jnp.float32), axis=1, keepdims=True)
    run_loop(1, n_ptl, lambda i: post_copy(i).wait_recv())

    def add_total(i):
        totbuf[...] += jnp.sum(post[i].astype(jnp.float32), axis=1, keepdims=True)

    run_loop(1, n_ptl, add_total)

    def other_sums(b):
        cols = pl.ds(pl.multiple_of(b * block, block), block)
        sums = sums_ref[:, cols]
        for i in range(1, n_ptl):
            images = gath[i, :, :, cols].reshape(n_lib * rows, block)
            sums = sums + jnp.dot(post[i], images, preferred_element_type=jnp.float32)
        sums_ref[:, cols] = sums

    lax.fori_loop(0, span // block, lambda b, c: (other_sums(b), c)[1], 0)

    own_total = total_ref.shape[0]
    total_ref[...] = totbuf[pl.ds(pl.multiple_of(ptl * own_total, 8), own_total), :]

    share = share_out[lib]
    for d in range(1, n_lib):
        share_copy(d).wait_recv()
        share = share + share_in[d - 1]
    share_ref[...] = share

    def ptl_sent(i):
        z_copy(i).wait_send()
        score_copy(i).wait_send()
        post_copy(i).wait_send()

    def lib_sent(d):
        stat_copy(d).wait_send()
        share_copy(d).wait_send()

    def spread_sent(i):
        run_loop(1, n_x, lambda d: x_copy(i, d).wait_send())
        run_loop(0, n_x, lambda d: core_copy(i, d).wait_send())

    run_loop(1, n_ptl, ptl_sent)
    run_loop(1, n_lib, lib_sent)
    run_loop(0, n_ptl, spread_sent)


def trig_table(half):
    index = np.arange(half)
    angle_x = (index % 64) * (2.0 * math.pi / 128.0)
    angle_y = (index // 64) * (2.0 * math.pi / 128.0)
    table = np.zeros((8, half), np.float32)
    table[0], table[1] = np.cos(angle_x), np.sin(angle_x)
    table[2], table[3] = np.cos(angle_y), np.sin(angle_y)
    return table


def on_device(n_lib, n_ptl, particles, shifts, references, inv_noise, proj_class):
    rows, width = particles.shape
    projections = references.shape[0]
    part_cols = width // n_ptl
    tiles = width // LANES
    cover = max(-(-(z * part_cols % LANES + part_cols) // LANES) for z in range(n_ptl))
    span = min(cover, tiles) * LANES
    n_x = n_lib // 2
    group = n_lib * rows
    own_total = projections // n_ptl
    vmem = pl.BlockSpec(memory_space=pltpu.VMEM)
    dma = pltpu.SemaphoreType.DMA
    sums, evidence, share, total = pl.pallas_call(
        functools.partial(kernel, n_lib, n_ptl, span),
        out_shape=(
            jax.ShapeDtypeStruct((projections, span), jnp.float32),
            jax.ShapeDtypeStruct((1, group), jnp.float32),
            jax.ShapeDtypeStruct((rows, CLASSES), jnp.float32),
            jax.ShapeDtypeStruct((own_total, 1), jnp.float32),
        ),
        in_specs=[vmem, vmem, vmem, pl.BlockSpec(memory_space=pl.ANY), vmem, vmem],
        out_specs=(vmem, vmem, vmem, vmem),
        scratch_shapes=[
            pltpu.VMEM((rows, width), jnp.bfloat16),
            pltpu.VMEM((n_ptl, n_lib, rows, span), jnp.bfloat16),
            pltpu.VMEM((projections, span), jnp.bfloat16),
            pltpu.VMEM((projections, span), jnp.bfloat16),
            pltpu.VMEM((n_ptl, projections, group), jnp.float32),
            pltpu.VMEM((n_ptl - 1, projections, group), jnp.float32),
            pltpu.VMEM((n_ptl, projections, group), jnp.bfloat16),
            pltpu.VMEM((8, group), jnp.float32),
            pltpu.VMEM((n_lib, 8, group), jnp.float32),
            pltpu.VMEM((n_lib, rows, CLASSES), jnp.float32),
            pltpu.VMEM((n_lib - 1, rows, CLASSES), jnp.float32),
            pltpu.VMEM((projections, 1), jnp.float32),
            dma,
            dma,
            dma((n_ptl - 1,)),
            dma((n_ptl - 1,)),
            dma((n_ptl, n_x - 1)),
            dma((n_ptl, n_x - 1)),
            dma((n_ptl, n_x)),
            dma((n_ptl, n_x)),
            dma((n_ptl - 1,)),
            dma((n_ptl - 1,)),
            dma((n_lib - 1,)),
            dma((n_lib - 1,)),
            dma((n_ptl - 1,)),
            dma((n_ptl - 1,)),
            dma((n_lib - 1,)),
            dma((n_lib - 1,)),
        ],
        compiler_params=pltpu.CompilerParams(
            collective_id=0, has_side_effects=True, vmem_limit_bytes=56 * 1024 * 1024
        ),
    )(
        particles,
        shifts[:, None],
        trig_table(width // 2),
        references,
        jnp.concatenate([inv_noise, inv_noise])[None, :],
        proj_class[:, None],
    )
    ptl, lib = lax.axis_index("ptl"), lax.axis_index("lib")
    first = jnp.minimum((ptl * part_cols) // LANES, tiles - span // LANES) * LANES
    out_sums = lax.dynamic_slice_in_dim(sums, ptl * part_cols - first, part_cols, 1)
    own_evidence = lax.dynamic_slice_in_dim(evidence[0], lib * rows, rows, 0)
    return own_evidence, share, out_sums, total[:, 0]


def solution(mesh):
    in_specs = (
        P(("grp", "lib", "ptl"), None),
        P(("grp", "lib", "ptl")),
        P(("grp", "lib"), None),
        P("grp"),
        P("lib"),
    )
    out_specs = (
        P(("grp", "lib", "ptl")),
        P(("grp", "lib", "ptl"), None),
        P(("grp", "lib"), "ptl"),
        P(("grp", "lib", "ptl")),
    )
    return jax.shard_map(
        functools.partial(on_device, mesh.shape["lib"], mesh.shape["ptl"]),
        mesh=mesh,
        in_specs=in_specs,
        out_specs=out_specs,
        check_vma=False,
    )
```

```python
import functools
import math

import jax
import jax.numpy as jnp
import numpy as np
from jax import lax
from jax.experimental import pallas as pl
from jax.experimental.pallas import tpu as pltpu
from jax.sharding import PartitionSpec as P

CLASSES = 16
WINDOW = 3
LANES = 128


def run_loop(low, high, body):
    if high - low <= 4:
        for index in range(low, high):
            body(index)
    else:

        def step(index, carry):
            body(index)
            return carry

        lax.fori_loop(low, high, step, 0)


def kernel(
    n_lib,
    n_ptl,
    span,
    pieces,
    window,
    part_ref,
    shift_ref,
    table_ref,
    refs_hbm,
    noise_ref,
    class_ref,
    sums_ref,
    evid_ref,
    share_ref,
    total_ref,
    noise2,
    shifted,
    gath,
    refbuf,
    weighted,
    spart,
    srecv,
    post,
    stat,
    stat_in,
    share_out,
    share_in,
    totbuf,
    ref_sem,
    own_sem,
    z_send,
    z_recv,
    x_send,
    x_recv,
    c_send,
    c_recv,
    s_send,
    s_recv,
    t_send,
    t_recv,
    p_send,
    p_recv,
    h_send,
    h_recv,
):
    lib = lax.axis_index("lib")
    ptl = lax.axis_index("ptl")
    n_x = n_lib // 2
    x, core = lib // 2, lib % 2
    mate = 2 * x + 1 - core
    rows, width = part_ref.shape
    half = width // 2
    part_cols = width // n_ptl
    tiles = width // LANES
    piece_rows = rows // pieces
    n_pieces = n_ptl * pieces

    def first_tile(z):
        return jnp.minimum((z * part_cols) // LANES, tiles - span // LANES)

    def chunk(z):
        return pl.ds(pl.multiple_of(first_tile(z) * LANES, LANES), span)

    barrier = pltpu.get_barrier_semaphore()

    def greet_ptl(step):
        pl.semaphore_signal(barrier, inc=1, device_id={"ptl": lax.rem(ptl + step, n_ptl)})

    def greet_lib(step):
        pl.semaphore_signal(barrier, inc=1, device_id={"lib": lax.rem(lib + step, n_lib)})

    run_loop(1, n_ptl, greet_ptl)
    run_loop(1, n_lib, greet_lib)

    ref_copy = pltpu.make_async_copy(refs_hbm.at[:, chunk(ptl)], refbuf, ref_sem)
    ref_copy.start()

    same = lax.broadcasted_iota(jnp.int32, (rows, rows), 0) == lax.broadcasted_iota(
        jnp.int32, (rows, rows), 1
    )
    ids = jnp.sum(
        jnp.where(same, shift_ref[...].astype(jnp.float32), 0.0), axis=1, keepdims=True
    ).astype(jnp.int32)
    step_y = (ids >= 3).astype(jnp.int32) + (ids >= 6).astype(jnp.int32)
    step_x = (ids - 3 * step_y - 1).astype(jnp.float32)
    step_y = (step_y - 1).astype(jnp.float32)
    cos_x = jnp.where(step_x == 0.0, 1.0, table_ref[0:1, 0:LANES])
    sin_x = step_x * table_ref[1:2, 0:LANES]
    for tile in range(half // LANES):
        lo = slice(tile * LANES, (tile + 1) * LANES)
        hi = slice(half + tile * LANES, half + (tile + 1) * LANES)
        cos_y = jnp.where(step_y == 0.0, 1.0, table_ref[2:3, lo])
        sin_y = step_y * table_ref[3:4, lo]
        cosine = cos_x * cos_y - sin_x * sin_y
        sine = sin_x * cos_y + cos_x * sin_y
        real = part_ref[:, lo].astype(jnp.float32)
        imag = part_ref[:, hi].astype(jnp.float32)
        shifted[:, lo] = (real * cosine + imag * sine).astype(jnp.bfloat16)
        shifted[:, hi] = (imag * cosine - real * sine).astype(jnp.bfloat16)

    pl.semaphore_wait(barrier, n_ptl - 1 + n_lib - 1)

    def part(i, source, r):
        return gath.at[i, source, pl.ds((r % pieces) * piece_rows, piece_rows)]

    def z_copy(r):
        to = lax.rem(ptl + r // pieces, n_ptl)
        return pltpu.make_async_remote_copy(
            src_ref=shifted.at[pl.ds((r % pieces) * piece_rows, piece_rows), chunk(to)],
            dst_ref=part(r // pieces, lib, r),
            send_sem=z_send.at[r - pieces],
            recv_sem=z_recv.at[r - pieces],
            device_id={"ptl": to},
        )

    for r in range(pieces, min(pieces + window, n_pieces)):
        z_copy(r).start()
    own_copy = pltpu.make_async_copy(shifted.at[:, chunk(ptl)], gath.at[0, lib], own_sem)
    own_copy.start()

    def x_source(d):
        return lax.rem(x - d + n_x, n_x) * 2 + core

    def lib_copy(r, d, source, send, recv, to):
        return pltpu.make_async_remote_copy(
            src_ref=part(r // pieces, source, r),
            dst_ref=part(r // pieces, source, r),
            send_sem=send.at[r, d],
            recv_sem=recv.at[r, d],
            device_id={"lib": to},
        )

    def x_copy(r, d):
        return lib_copy(r, d - 1, lib, x_send, x_recv, lax.rem(x + d, n_x) * 2 + core)

    def x_arrival(r, d):
        return lib_copy(r, d - 1, x_source(d), x_send, x_recv, x_source(d))

    def core_copy(r, d):
        return lib_copy(r, d, x_source(d), c_send, c_recv, mate)

    def core_arrival(r, d):
        return lib_copy(r, d, x_source(d) + 1 - 2 * core, c_send, c_recv, mate)

    def z_arrival(r):
        return pltpu.make_async_remote_copy(
            src_ref=part(r // pieces, lib, r),
            dst_ref=part(r // pieces, lib, r),
            send_sem=z_send.at[r - pieces],
            recv_sem=z_recv.at[r - pieces],
            device_id={"ptl": lax.rem(ptl - r // pieces + n_ptl, n_ptl)},
        )

    def spread(r):
        run_loop(1, n_x, lambda d: x_copy(r, d).start())
        core_copy(r, 0).start()

    def score_copy(i):
        return pltpu.make_async_remote_copy(
            src_ref=spart.at[i],
            dst_ref=srecv.at[i - 1],
            send_sem=s_send.at[i - 1],
            recv_sem=s_recv.at[i - 1],
            device_id={"ptl": lax.rem(ptl - i + n_ptl, n_ptl)},
        )

    def relay(r):
        def forward(d):
            x_arrival(r, d).wait_recv()
            core_copy(r, d).start()

        run_loop(1, n_x, forward)

    def score(i):
        for p in range(pieces):
            run_loop(0, n_x, lambda d: core_arrival(i * pieces + p, d).wait_recv())
        block = gath[i].reshape(n_lib * rows, span)
        spart[i] = (
            lax.dot_general(
                weighted[...], block, (((1,), (1,)), ((), ())), preferred_element_type=jnp.float32
            )
            - half_norm
        )

    own_copy.wait()
    for r in range(pieces):
        spread(r)

    noise2[:, 0:half] = noise_ref[...]
    noise2[:, half:width] = noise_ref[...]

    ref_copy.wait()
    offset = ptl * part_cols - first_tile(ptl) * LANES
    place = lax.broadcasted_iota(jnp.int32, (1, span), 1)
    inside = (place >= offset) & (place < offset + part_cols)
    noise = jnp.where(inside, noise2[:, chunk(ptl)], 0.0)
    widened = refbuf[...].astype(jnp.float32)
    scaled = widened * noise
    weighted[...] = scaled.astype(jnp.bfloat16)
    half_norm = 0.5 * jnp.sum(widened * scaled, axis=1, keepdims=True)

    lag = min(2, pieces)
    for r in range(pieces - lag):
        relay(r)

    def group(i):
        for p in range(pieces):
            r = i * pieces + p
            z_arrival(r).wait_recv()
            spread(r)

            @pl.when(r + window < n_pieces)
            def _():
                z_copy(r + window).start()

            relay(r - lag)
        score(i - 1)

    group(1)

    def middle(i):
        group(i)
        score_copy(i - 1).start()

    run_loop(2, n_ptl, middle)
    for r in range(n_pieces - lag, n_pieces):
        relay(r)
    score(n_ptl - 1)
    score_copy(n_ptl - 1).start()

    def add_scores(i):
        score_copy(i).wait_recv()
        spart[0] = spart[0] + srecv[i - 1]

    run_loop(1, n_ptl, add_scores)
    scores = spart[0]

    peak = jnp.max(scores, axis=0, keepdims=True)
    stat[0:1] = peak
    stat[1:2] = jnp.sum(jnp.exp(scores - peak), axis=0, keepdims=True)

    def stat_copy(d):
        return pltpu.make_async_remote_copy(
            src_ref=stat,
            dst_ref=stat_in.at[d],
            send_sem=t_send.at[d - 1],
            recv_sem=t_recv.at[d - 1],
            device_id={"lib": lax.rem(lib + d, n_lib)},
        )

    run_loop(1, n_lib, lambda d: stat_copy(d).start())
    stat_in[0, 0:2] = stat[0:2]
    run_loop(1, n_lib, lambda d: stat_copy(d).wait_recv())
    top = peak
    for d in range(1, n_lib):
        top = jnp.maximum(top, stat_in[d, 0:1])
    total = jnp.zeros_like(top)
    for d in range(n_lib):
        total = total + stat_in[d, 1:2] * jnp.exp(stat_in[d, 0:1] - top)
    evidence = top + jnp.log(total)
    own_evidence = evidence[:, 0:rows]
    for l in range(1, n_lib):
        own_evidence = jnp.where(lib == l, evidence[:, l * rows : (l + 1) * rows], own_evidence)
    evid_ref[...] = own_evidence
    own_post = jnp.exp(scores - evidence).astype(jnp.bfloat16)
    post[0] = own_post

    def post_copy(i):
        return pltpu.make_async_remote_copy(
            src_ref=post.at[0],
            dst_ref=post.at[i],
            send_sem=p_send.at[i - 1],
            recv_sem=p_recv.at[i - 1],
            device_id={"ptl": lax.rem(ptl + i, n_ptl)},
        )

    run_loop(1, n_ptl, lambda i: post_copy(i).start())

    onehot = (
        class_ref[...] == lax.broadcasted_iota(jnp.int32, (CLASSES, class_ref.shape[1]), 0)
    ).astype(jnp.bfloat16)
    share_out[...] = lax.dot_general(
        own_post, onehot, (((0,), (1,)), ((), ())), preferred_element_type=jnp.float32
    ).reshape(n_lib, rows, CLASSES)

    def share_copy(d):
        to = lax.rem(lib + d, n_lib)
        return pltpu.make_async_remote_copy(
            src_ref=share_out.at[to],
            dst_ref=share_in.at[d - 1],
            send_sem=h_send.at[d - 1],
            recv_sem=h_recv.at[d - 1],
            device_id={"lib": to},
        )

    run_loop(1, n_lib, lambda d: share_copy(d).start())

    block = 512 if span % 512 == 0 else LANES

    def own_sums(b):
        cols = pl.ds(pl.multiple_of(b * block, block), block)
        images = gath[0, :, :, cols].reshape(n_lib * rows, block)
        sums_ref[:, cols] = jnp.dot(own_post, images, preferred_element_type=jnp.float32)

    lax.fori_loop(0, span // block, lambda b, c: (own_sums(b), c)[1], 0)

    ones = jnp.ones((8, n_lib * rows), jnp.bfloat16)

    def totals(weights):
        return lax.dot_general(
            ones, weights, (((1,), (1,)), ((), ())), preferred_element_type=jnp.float32
        )

    totbuf[...] = totals(own_post)
    run_loop(1, n_ptl, lambda i: post_copy(i).wait_recv())

    def add_total(i):
        totbuf[...] += totals(post[i])

    run_loop(1, n_ptl, add_total)

    def other_sums(b):
        cols = pl.ds(pl.multiple_of(b * block, block), block)
        sums = sums_ref[:, cols]
        for i in range(1, n_ptl):
            images = gath[i, :, :, cols].reshape(n_lib * rows, block)
            sums = sums + jnp.dot(post[i], images, preferred_element_type=jnp.float32)
        sums_ref[:, cols] = sums

    lax.fori_loop(0, span // block, lambda b, c: (other_sums(b), c)[1], 0)

    count = total_ref.shape[1]
    own_total = totbuf[0:1, 0:count]
    for z in range(1, n_ptl):
        own_total = jnp.where(ptl == z, totbuf[0:1, z * count : (z + 1) * count], own_total)
    total_ref[...] = own_total

    share = share_out[lib]
    for d in range(1, n_lib):
        share_copy(d).wait_recv()
        share = share + share_in[d - 1]
    share_ref[...] = share

    def ptl_sent(i):
        score_copy(i).wait_send()
        post_copy(i).wait_send()

    def lib_sent(d):
        stat_copy(d).wait_send()
        share_copy(d).wait_send()

    def spread_sent(r):
        run_loop(1, n_x, lambda d: x_copy(r, d).wait_send())
        run_loop(0, n_x, lambda d: core_copy(r, d).wait_send())

    run_loop(1, n_ptl, ptl_sent)
    run_loop(1, n_lib, lib_sent)
    run_loop(pieces, n_pieces, lambda r: z_copy(r).wait_send())
    run_loop(0, n_pieces, spread_sent)


def finish(n_ptl, part_cols, sums_in, evid_in, share_in, total_in, sums, evid, share, total):
    span = sums_in.shape[1]
    z = lax.axis_index("ptl")
    tiles = n_ptl * part_cols // LANES
    offset = z * part_cols - jnp.minimum((z * part_cols) // LANES, tiles - span // LANES) * LANES
    turned = pltpu.roll(sums_in[...], lax.rem(span - offset, span), 1)
    sums[...] = turned[:, 0:part_cols]
    evid[...] = evid_in[...]
    share[...] = share_in[...]
    total[...] = total_in[...]


def trig_table(half):
    index = np.arange(half)
    angle_x = (index % 64) * (2.0 * math.pi / 128.0)
    angle_y = (index // 64) * (2.0 * math.pi / 128.0)
    table = np.zeros((8, half), np.float32)
    table[0], table[1] = np.cos(angle_x), np.sin(angle_x)
    table[2], table[3] = np.cos(angle_y), np.sin(angle_y)
    return table


def on_device(n_lib, n_ptl, particles, shifts, references, inv_noise, proj_class):
    rows, width = particles.shape
    projections = references.shape[0]
    part_cols = width // n_ptl
    tiles = width // LANES
    cover = max(-(-(z * part_cols % LANES + part_cols) // LANES) for z in range(n_ptl))
    span = min(cover, tiles) * LANES
    n_x = n_lib // 2
    group = n_lib * rows
    own_total = projections // n_ptl
    pieces = 3 if rows % 48 == 0 else 1
    window = WINDOW
    n_pieces = n_ptl * pieces
    vmem = pl.BlockSpec(memory_space=pltpu.VMEM)
    dma = pltpu.SemaphoreType.DMA
    sums, evidence, share, total = pl.pallas_call(
        functools.partial(kernel, n_lib, n_ptl, span, pieces, window),
        out_shape=(
            jax.ShapeDtypeStruct((projections, span), jnp.float32),
            jax.ShapeDtypeStruct((1, rows), jnp.float32),
            jax.ShapeDtypeStruct((rows, CLASSES), jnp.float32),
            jax.ShapeDtypeStruct((1, own_total), jnp.float32),
        ),
        in_specs=[vmem, vmem, vmem, pl.BlockSpec(memory_space=pl.ANY), vmem, vmem],
        out_specs=(vmem, vmem, vmem, vmem),
        scratch_shapes=[
            pltpu.VMEM((1, width), jnp.float32),
            pltpu.VMEM((rows, width), jnp.bfloat16),
            pltpu.VMEM((n_ptl, n_lib, rows, span), jnp.bfloat16),
            pltpu.VMEM((projections, span), jnp.bfloat16),
            pltpu.VMEM((projections, span), jnp.bfloat16),
            pltpu.VMEM((n_ptl, projections, group), jnp.float32),
            pltpu.VMEM((n_ptl - 1, projections, group), jnp.float32),
            pltpu.VMEM((n_ptl, projections, group), jnp.bfloat16),
            pltpu.VMEM((8, group), jnp.float32),
            pltpu.VMEM((n_lib, 8, group), jnp.float32),
            pltpu.VMEM((n_lib, rows, CLASSES), jnp.float32),
            pltpu.VMEM((n_lib - 1, rows, CLASSES), jnp.float32),
            pltpu.VMEM((8, projections), jnp.float32),
            dma,
            dma,
            dma((n_pieces - pieces,)),
            dma((n_pieces - pieces,)),
            dma((n_pieces, n_x - 1)),
            dma((n_pieces, n_x - 1)),
            dma((n_pieces, n_x)),
            dma((n_pieces, n_x)),
            dma((n_ptl - 1,)),
            dma((n_ptl - 1,)),
            dma((n_lib - 1,)),
            dma((n_lib - 1,)),
            dma((n_ptl - 1,)),
            dma((n_ptl - 1,)),
            dma((n_lib - 1,)),
            dma((n_lib - 1,)),
        ],
        compiler_params=pltpu.CompilerParams(
            collective_id=0, has_side_effects=True, vmem_limit_bytes=56 * 1024 * 1024
        ),
    )(
        particles,
        shifts[None, :],
        trig_table(width // 2),
        references,
        inv_noise[None, :],
        proj_class[None, :],
    )
    block = projections // 4

    def fixed(shape):
        return pl.BlockSpec(shape, lambda i: (0, 0))

    small = [fixed((1, rows)), fixed((rows, CLASSES)), fixed((1, own_total))]
    sums, evidence, share, total = pl.pallas_call(
        functools.partial(finish, n_ptl, part_cols),
        grid=(4,),
        out_shape=(
            jax.ShapeDtypeStruct((projections, part_cols), jnp.float32),
            jax.ShapeDtypeStruct((1, rows), jnp.float32),
            jax.ShapeDtypeStruct((rows, CLASSES), jnp.float32),
            jax.ShapeDtypeStruct((1, own_total), jnp.float32),
        ),
        in_specs=[pl.BlockSpec((block, span), lambda i: (i, 0))] + small,
        out_specs=tuple([pl.BlockSpec((block, part_cols), lambda i: (i, 0))] + small),
    )(sums, evidence, share, total)
    return evidence[0], share, sums, total[0]


def solution(mesh):
    in_specs = (
        P(("grp", "lib", "ptl"), None),
        P(("grp", "lib", "ptl")),
        P(("grp", "lib"), None),
        P("grp"),
        P("lib"),
    )
    out_specs = (
        P(("grp", "lib", "ptl")),
        P(("grp", "lib", "ptl"), None),
        P(("grp", "lib"), "ptl"),
        P(("grp", "lib", "ptl")),
    )
    return jax.shard_map(
        functools.partial(on_device, mesh.shape["lib"], mesh.shape["ptl"]),
        mesh=mesh,
        in_specs=in_specs,
        out_specs=out_specs,
        check_vma=False,
    )
```

```python
import functools
import math

import jax
import jax.numpy as jnp
import numpy as np
from jax import lax
from jax.experimental import pallas as pl
from jax.experimental.pallas import tpu as pltpu
from jax.sharding import PartitionSpec as P

CLASSES = 16
WINDOW = 3
LANES = 128


def run_loop(low, high, body):
    if high - low <= 4:
        for index in range(low, high):
            body(index)
    else:

        def step(index, carry):
            body(index)
            return carry

        lax.fori_loop(low, high, step, 0)


def diagonal(count):
    shape = (count, count)
    return lax.broadcasted_iota(jnp.int32, shape, 0) == lax.broadcasted_iota(jnp.int32, shape, 1)


def to_column(row):
    return jnp.sum(jnp.where(diagonal(row.shape[1]), row, 0.0), axis=1, keepdims=True)


def to_row(column):
    return jnp.sum(jnp.where(diagonal(column.shape[0]), column, 0.0), axis=0, keepdims=True)


def kernel(
    n_lib,
    n_ptl,
    span,
    pieces,
    window,
    part_ref,
    shift_ref,
    table_ref,
    refs_hbm,
    noise_ref,
    class_ref,
    sums_ref,
    evid_ref,
    share_ref,
    total_ref,
    noise2,
    shifted,
    gath,
    refbuf,
    weighted,
    spart,
    srecv,
    post,
    stat,
    stat_in,
    share_out,
    share_in,
    totbuf,
    own_part,
    ref_sem,
    own_sem,
    z_send,
    z_recv,
    x_send,
    x_recv,
    c_send,
    c_recv,
    s_send,
    s_recv,
    t_send,
    t_recv,
    p_send,
    p_recv,
    h_send,
    h_recv,
):
    lib = lax.axis_index("lib")
    ptl = lax.axis_index("ptl")
    n_x = n_lib // 2
    x, core = lib // 2, lib % 2
    mate = 2 * x + 1 - core
    rows, width = part_ref.shape
    half = width // 2
    part_cols = width // n_ptl
    tiles = width // LANES
    piece_rows = rows // pieces
    n_pieces = n_ptl * pieces

    def first_tile(z):
        return jnp.minimum((z * part_cols) // LANES, tiles - span // LANES)

    def chunk(z):
        return pl.ds(pl.multiple_of(first_tile(z) * LANES, LANES), span)

    barrier = pltpu.get_barrier_semaphore()

    def greet_ptl(step):
        pl.semaphore_signal(barrier, inc=1, device_id={"ptl": lax.rem(ptl + step, n_ptl)})

    def greet_lib(step):
        pl.semaphore_signal(barrier, inc=1, device_id={"lib": lax.rem(lib + step, n_lib)})

    run_loop(1, n_ptl, greet_ptl)
    run_loop(1, n_lib, greet_lib)

    ref_copy = pltpu.make_async_copy(refs_hbm.at[:, chunk(ptl)], refbuf, ref_sem)
    ref_copy.start()

    ids = to_column(shift_ref[...].astype(jnp.float32)).astype(jnp.int32)
    step_y = (ids >= 3).astype(jnp.int32) + (ids >= 6).astype(jnp.int32)
    step_x = (ids - 3 * step_y - 1).astype(jnp.float32)
    step_y = (step_y - 1).astype(jnp.float32)
    cos_x = jnp.where(step_x == 0.0, 1.0, table_ref[0:1, 0:LANES])
    sin_x = step_x * table_ref[1:2, 0:LANES]
    for tile in range(half // LANES):
        lo = slice(tile * LANES, (tile + 1) * LANES)
        hi = slice(half + tile * LANES, half + (tile + 1) * LANES)
        cos_y = jnp.where(step_y == 0.0, 1.0, table_ref[2:3, lo])
        sin_y = step_y * table_ref[3:4, lo]
        cosine = cos_x * cos_y - sin_x * sin_y
        sine = sin_x * cos_y + cos_x * sin_y
        real = part_ref[:, lo].astype(jnp.float32)
        imag = part_ref[:, hi].astype(jnp.float32)
        shifted[:, lo] = (real * cosine + imag * sine).astype(jnp.bfloat16)
        shifted[:, hi] = (imag * cosine - real * sine).astype(jnp.bfloat16)

    pl.semaphore_wait(barrier, n_ptl - 1 + n_lib - 1)

    def part(i, source, r):
        return gath.at[i, source, pl.ds((r % pieces) * piece_rows, piece_rows)]

    def z_copy(r):
        to = lax.rem(ptl + r // pieces, n_ptl)
        return pltpu.make_async_remote_copy(
            src_ref=shifted.at[pl.ds((r % pieces) * piece_rows, piece_rows), chunk(to)],
            dst_ref=part(r // pieces, lib, r),
            send_sem=z_send.at[r - pieces],
            recv_sem=z_recv.at[r - pieces],
            device_id={"ptl": to},
        )

    for r in range(pieces, min(pieces + window, n_pieces)):
        z_copy(r).start()
    own_copy = pltpu.make_async_copy(shifted.at[:, chunk(ptl)], gath.at[0, lib], own_sem)
    own_copy.start()

    def x_source(d):
        return lax.rem(x - d + n_x, n_x) * 2 + core

    def lib_copy(r, d, source, send, recv, to):
        return pltpu.make_async_remote_copy(
            src_ref=part(r // pieces, source, r),
            dst_ref=part(r // pieces, source, r),
            send_sem=send.at[r, d],
            recv_sem=recv.at[r, d],
            device_id={"lib": to},
        )

    def x_copy(r, d):
        return lib_copy(r, d - 1, lib, x_send, x_recv, lax.rem(x + d, n_x) * 2 + core)

    def x_arrival(r, d):
        return lib_copy(r, d - 1, x_source(d), x_send, x_recv, x_source(d))

    def core_copy(r, d):
        return lib_copy(r, d, x_source(d), c_send, c_recv, mate)

    def core_arrival(r, d):
        return lib_copy(r, d, x_source(d) + 1 - 2 * core, c_send, c_recv, mate)

    def z_arrival(r):
        return pltpu.make_async_remote_copy(
            src_ref=part(r // pieces, lib, r),
            dst_ref=part(r // pieces, lib, r),
            send_sem=z_send.at[r - pieces],
            recv_sem=z_recv.at[r - pieces],
            device_id={"ptl": lax.rem(ptl - r // pieces + n_ptl, n_ptl)},
        )

    def spread(r):
        run_loop(1, n_x, lambda d: x_copy(r, d).start())
        core_copy(r, 0).start()

    def score_copy(i):
        return pltpu.make_async_remote_copy(
            src_ref=spart.at[i],
            dst_ref=srecv.at[i - 1],
            send_sem=s_send.at[i - 1],
            recv_sem=s_recv.at[i - 1],
            device_id={"ptl": lax.rem(ptl - i + n_ptl, n_ptl)},
        )

    def relay(r):
        def forward(d):
            x_arrival(r, d).wait_recv()
            core_copy(r, d).start()

        run_loop(1, n_x, forward)

    def score(i):
        for p in range(pieces):
            run_loop(0, n_x, lambda d: core_arrival(i * pieces + p, d).wait_recv())
        block = gath[i].reshape(n_lib * rows, span)
        spart[i] = (
            lax.dot_general(
                block, weighted[...], (((1,), (1,)), ((), ())), preferred_element_type=jnp.float32
            )
            - half_norm
        )

    own_copy.wait()
    for r in range(pieces):
        spread(r)

    noise2[:, 0:half] = noise_ref[...]
    noise2[:, half:width] = noise_ref[...]

    ref_copy.wait()
    offset = ptl * part_cols - first_tile(ptl) * LANES
    place = lax.broadcasted_iota(jnp.int32, (1, span), 1)
    inside = (place >= offset) & (place < offset + part_cols)
    noise = jnp.where(inside, noise2[:, chunk(ptl)], 0.0)
    widened = refbuf[...].astype(jnp.float32)
    scaled = widened * noise
    weighted[...] = scaled.astype(jnp.bfloat16)
    half_norm = to_row(0.5 * jnp.sum(widened * scaled, axis=1, keepdims=True))

    lag = min(2, pieces)
    for r in range(pieces - lag):
        relay(r)

    def group(i):
        for p in range(pieces):
            r = i * pieces + p
            z_arrival(r).wait_recv()
            spread(r)

            @pl.when(r + window < n_pieces)
            def _():
                z_copy(r + window).start()

            relay(r - lag)
        score(i - 1)

    group(1)

    def middle(i):
        group(i)
        score_copy(i - 1).start()

    run_loop(2, n_ptl, middle)
    for r in range(n_pieces - lag, n_pieces):
        relay(r)
    score(n_ptl - 1)
    score_copy(n_ptl - 1).start()

    def add_scores(i):
        score_copy(i).wait_recv()
        spart[0] = spart[0] + srecv[i - 1]

    run_loop(1, n_ptl, add_scores)
    scores = spart[0]

    own_peak = jnp.max(scores, axis=1, keepdims=True)
    peak = to_row(own_peak)
    stat[0:1] = peak
    stat[1:2] = to_row(jnp.sum(jnp.exp(scores - own_peak), axis=1, keepdims=True))

    def stat_copy(d):
        return pltpu.make_async_remote_copy(
            src_ref=stat,
            dst_ref=stat_in.at[d],
            send_sem=t_send.at[d - 1],
            recv_sem=t_recv.at[d - 1],
            device_id={"lib": lax.rem(lib + d, n_lib)},
        )

    run_loop(1, n_lib, lambda d: stat_copy(d).start())
    stat_in[0, 0:2] = stat[0:2]
    run_loop(1, n_lib, lambda d: stat_copy(d).wait_recv())
    top = peak
    for d in range(1, n_lib):
        top = jnp.maximum(top, stat_in[d, 0:1])
    total = jnp.zeros_like(top)
    for d in range(n_lib):
        total = total + stat_in[d, 1:2] * jnp.exp(stat_in[d, 0:1] - top)
    evidence = top + jnp.log(total)
    own_evidence = evidence[:, 0:rows]
    for l in range(1, n_lib):
        own_evidence = jnp.where(lib == l, evidence[:, l * rows : (l + 1) * rows], own_evidence)
    evid_ref[...] = own_evidence
    own_post = jnp.exp(scores - to_column(evidence)).astype(jnp.bfloat16)
    post[0] = own_post

    def post_copy(i):
        return pltpu.make_async_remote_copy(
            src_ref=post.at[0],
            dst_ref=post.at[i],
            send_sem=p_send.at[i - 1],
            recv_sem=p_recv.at[i - 1],
            device_id={"ptl": lax.rem(ptl + i, n_ptl)},
        )

    run_loop(1, n_ptl, lambda i: post_copy(i).start())

    onehot = (
        class_ref[...] == lax.broadcasted_iota(jnp.int32, (CLASSES, class_ref.shape[1]), 0)
    ).astype(jnp.bfloat16)
    shares = lax.dot_general(
        onehot, own_post, (((1,), (1,)), ((), ())), preferred_element_type=jnp.float32
    )
    for l in range(n_lib):
        share_out[l] = shares[:, l * rows : (l + 1) * rows]

    def share_copy(d):
        to = lax.rem(lib + d, n_lib)
        return pltpu.make_async_remote_copy(
            src_ref=share_out.at[to],
            dst_ref=share_in.at[d - 1],
            send_sem=h_send.at[d - 1],
            recv_sem=h_recv.at[d - 1],
            device_id={"lib": to},
        )

    run_loop(1, n_lib, lambda d: share_copy(d).start())

    def weigh(weights, images):
        return lax.dot_general(
            weights, images, (((0,), (0,)), ((), ())), preferred_element_type=jnp.float32
        )

    block = 512 if span % 512 == 0 else LANES

    def own_sums(b):
        cols = pl.ds(pl.multiple_of(b * block, block), block)
        images = gath[0, :, :, cols].reshape(n_lib * rows, block)
        own_part[:, cols] = weigh(own_post, images)

    lax.fori_loop(0, span // block, lambda b, c: (own_sums(b), c)[1], 0)

    ones = jnp.ones((8, n_lib * rows), jnp.bfloat16)

    def totals(weights):
        return lax.dot_general(
            ones, weights, (((1,), (0,)), ((), ())), preferred_element_type=jnp.float32
        )

    totbuf[...] = totals(own_post)
    run_loop(1, n_ptl, lambda i: post_copy(i).wait_recv())

    def add_total(i):
        totbuf[...] += totals(post[i])

    run_loop(1, n_ptl, add_total)

    def other_sums(b):
        cols = pl.ds(pl.multiple_of(b * block, block), block)
        sums = own_part[:, cols]
        for i in range(1, n_ptl):
            images = gath[i, :, :, cols].reshape(n_lib * rows, block)
            sums = sums + weigh(post[i], images)
        sums_ref[cols, :] = sums.T

    lax.fori_loop(0, span // block, lambda b, c: (other_sums(b), c)[1], 0)

    count = total_ref.shape[1]
    own_total = totbuf[0:1, 0:count]
    for z in range(1, n_ptl):
        own_total = jnp.where(ptl == z, totbuf[0:1, z * count : (z + 1) * count], own_total)
    total_ref[...] = own_total

    share = share_out[lib]
    for d in range(1, n_lib):
        share_copy(d).wait_recv()
        share = share + share_in[d - 1]
    share_ref[...] = share

    def ptl_sent(i):
        score_copy(i).wait_send()
        post_copy(i).wait_send()

    def lib_sent(d):
        stat_copy(d).wait_send()
        share_copy(d).wait_send()

    def spread_sent(r):
        run_loop(1, n_x, lambda d: x_copy(r, d).wait_send())
        run_loop(0, n_x, lambda d: core_copy(r, d).wait_send())

    run_loop(1, n_ptl, ptl_sent)
    run_loop(1, n_lib, lib_sent)
    run_loop(pieces, n_pieces, lambda r: z_copy(r).wait_send())
    run_loop(0, n_pieces, spread_sent)


def finish(n_ptl, sums_in, evid_in, share_in, total_in, sums, evid, share, total, sem):
    part_cols = sums.shape[0]
    span = sums_in.shape[0]
    z = lax.axis_index("ptl")
    tiles = n_ptl * part_cols // LANES
    offset = z * part_cols - jnp.minimum((z * part_cols) // LANES, tiles - span // LANES) * LANES
    copy = pltpu.make_async_copy(
        sums_in.at[pl.ds(pl.multiple_of(offset, 8), part_cols)], sums, sem
    )
    copy.start()
    evid[...] = evid_in[...]
    share[...] = share_in[...]
    total[...] = total_in[...]
    copy.wait()


def trig_table(half):
    index = np.arange(half)
    angle_x = (index % 64) * (2.0 * math.pi / 128.0)
    angle_y = (index // 64) * (2.0 * math.pi / 128.0)
    table = np.zeros((8, half), np.float32)
    table[0], table[1] = np.cos(angle_x), np.sin(angle_x)
    table[2], table[3] = np.cos(angle_y), np.sin(angle_y)
    return table


def on_device(n_lib, n_ptl, particles, shifts, references, inv_noise, proj_class):
    rows, width = particles.shape
    projections = references.shape[0]
    part_cols = width // n_ptl
    tiles = width // LANES
    cover = max(-(-(z * part_cols % LANES + part_cols) // LANES) for z in range(n_ptl))
    span = min(cover, tiles) * LANES
    n_x = n_lib // 2
    group = n_lib * rows
    own_total = projections // n_ptl
    pieces = 3 if rows % 48 == 0 else 1
    window = WINDOW
    n_pieces = n_ptl * pieces
    vmem = pl.BlockSpec(memory_space=pltpu.VMEM)
    dma = pltpu.SemaphoreType.DMA
    sums, evidence, share, total = pl.pallas_call(
        functools.partial(kernel, n_lib, n_ptl, span, pieces, window),
        out_shape=(
            jax.ShapeDtypeStruct((span, projections), jnp.float32),
            jax.ShapeDtypeStruct((1, rows), jnp.float32),
            jax.ShapeDtypeStruct((CLASSES, rows), jnp.float32),
            jax.ShapeDtypeStruct((1, own_total), jnp.float32),
        ),
        in_specs=[vmem, vmem, vmem, pl.BlockSpec(memory_space=pl.ANY), vmem, vmem],
        out_specs=(vmem, vmem, vmem, vmem),
        scratch_shapes=[
            pltpu.VMEM((1, width), jnp.float32),
            pltpu.VMEM((rows, width), jnp.bfloat16),
            pltpu.VMEM((n_ptl, n_lib, rows, span), jnp.bfloat16),
            pltpu.VMEM((projections, span), jnp.bfloat16),
            pltpu.VMEM((projections, span), jnp.bfloat16),
            pltpu.VMEM((n_ptl, group, projections), jnp.float32),
            pltpu.VMEM((n_ptl - 1, group, projections), jnp.float32),
            pltpu.VMEM((n_ptl, group, projections), jnp.bfloat16),
            pltpu.VMEM((8, group), jnp.float32),
            pltpu.VMEM((n_lib, 8, group), jnp.float32),
            pltpu.VMEM((n_lib, CLASSES, rows), jnp.float32),
            pltpu.VMEM((n_lib - 1, CLASSES, rows), jnp.float32),
            pltpu.VMEM((8, projections), jnp.float32),
            pltpu.VMEM((projections, span), jnp.float32),
            dma,
            dma,
            dma((n_pieces - pieces,)),
            dma((n_pieces - pieces,)),
            dma((n_pieces, n_x - 1)),
            dma((n_pieces, n_x - 1)),
            dma((n_pieces, n_x)),
            dma((n_pieces, n_x)),
            dma((n_ptl - 1,)),
            dma((n_ptl - 1,)),
            dma((n_lib - 1,)),
            dma((n_lib - 1,)),
            dma((n_ptl - 1,)),
            dma((n_ptl - 1,)),
            dma((n_lib - 1,)),
            dma((n_lib - 1,)),
        ],
        compiler_params=pltpu.CompilerParams(
            collective_id=0, has_side_effects=True, vmem_limit_bytes=56 * 1024 * 1024
        ),
    )(
        particles,
        shifts[None, :],
        trig_table(width // 2),
        references,
        inv_noise[None, :],
        proj_class[None, :],
    )
    far = pl.BlockSpec(memory_space=pl.ANY)
    sums, evidence, share, total = pl.pallas_call(
        functools.partial(finish, n_ptl),
        out_shape=(
            jax.ShapeDtypeStruct((part_cols, projections), jnp.float32),
            jax.ShapeDtypeStruct((1, rows), jnp.float32),
            jax.ShapeDtypeStruct((CLASSES, rows), jnp.float32),
            jax.ShapeDtypeStruct((1, own_total), jnp.float32),
        ),
        in_specs=[far, vmem, vmem, vmem],
        out_specs=(far, vmem, vmem, vmem),
        scratch_shapes=[dma],
    )(sums, evidence, share, total)
    return evidence[0], share.T, sums.T, total[0]


def solution(mesh):
    in_specs = (
        P(("grp", "lib", "ptl"), None),
        P(("grp", "lib", "ptl")),
        P(("grp", "lib"), None),
        P("grp"),
        P("lib"),
    )
    out_specs = (
        P(("grp", "lib", "ptl")),
        P(("grp", "lib", "ptl"), None),
        P(("grp", "lib"), "ptl"),
        P(("grp", "lib", "ptl")),
    )
    return jax.shard_map(
        functools.partial(on_device, mesh.shape["lib"], mesh.shape["ptl"]),
        mesh=mesh,
        in_specs=in_specs,
        out_specs=out_specs,
        check_vma=False,
    )
```

```python
import functools
import math

import jax
import jax.numpy as jnp
import numpy as np
from jax import lax
from jax.experimental import pallas as pl
from jax.experimental.pallas import tpu as pltpu
from jax.sharding import PartitionSpec as P

CLASSES = 16
WINDOW = 3
LANES = 128


def run_loop(low, high, body):
    if high - low <= 4:
        for index in range(low, high):
            body(index)
    else:

        def step(index, carry):
            body(index)
            return carry

        lax.fori_loop(low, high, step, 0)


def hop(index, count):
    odd = index % 2
    return odd * ((index + 1) // 2) + (1 - odd) * (count - index // 2)


def diagonal(count):
    shape = (count, count)
    return lax.broadcasted_iota(jnp.int32, shape, 0) == lax.broadcasted_iota(jnp.int32, shape, 1)


def to_column(row):
    return jnp.sum(jnp.where(diagonal(row.shape[1]), row, 0.0), axis=1, keepdims=True)


def to_row(column):
    return jnp.sum(jnp.where(diagonal(column.shape[0]), column, 0.0), axis=0, keepdims=True)


def kernel(
    n_lib,
    n_ptl,
    span,
    pieces,
    window,
    part_ref,
    shift_ref,
    table_ref,
    refs_hbm,
    noise_ref,
    class_ref,
    sums_ref,
    evid_ref,
    share_ref,
    total_ref,
    noise2,
    shifted,
    gath,
    refbuf,
    weighted,
    spart,
    srecv,
    post,
    stat,
    stat_in,
    share_out,
    share_in,
    totbuf,
    own_part,
    ref_sem,
    own_sem,
    z_send,
    z_recv,
    x_send,
    x_recv,
    c_send,
    c_recv,
    s_send,
    s_recv,
    t_send,
    t_recv,
    p_send,
    p_recv,
    h_send,
    h_recv,
):
    lib = lax.axis_index("lib")
    ptl = lax.axis_index("ptl")
    n_x = n_lib // 2
    x, core = lib // 2, lib % 2
    mate = 2 * x + 1 - core
    rows, width = part_ref.shape
    half = width // 2
    part_cols = width // n_ptl
    tiles = width // LANES
    piece_rows = rows // pieces
    n_pieces = n_ptl * pieces

    def first_tile(z):
        return jnp.minimum((z * part_cols) // LANES, tiles - span // LANES)

    def chunk(z):
        return pl.ds(pl.multiple_of(first_tile(z) * LANES, LANES), span)

    barrier = pltpu.get_barrier_semaphore()

    def greet_ptl(step):
        pl.semaphore_signal(barrier, inc=1, device_id={"ptl": lax.rem(ptl + step, n_ptl)})

    def greet_lib(step):
        pl.semaphore_signal(barrier, inc=1, device_id={"lib": lax.rem(lib + step, n_lib)})

    run_loop(1, n_ptl, greet_ptl)
    run_loop(1, n_lib, greet_lib)

    ref_copy = pltpu.make_async_copy(refs_hbm.at[:, chunk(ptl)], refbuf, ref_sem)
    ref_copy.start()

    ids = to_column(shift_ref[...].astype(jnp.float32)).astype(jnp.int32)
    step_y = (ids >= 3).astype(jnp.int32) + (ids >= 6).astype(jnp.int32)
    step_x = (ids - 3 * step_y - 1).astype(jnp.float32)
    step_y = (step_y - 1).astype(jnp.float32)
    cos_x = jnp.where(step_x == 0.0, 1.0, table_ref[0:1, 0:LANES])
    sin_x = step_x * table_ref[1:2, 0:LANES]
    for tile in range(half // LANES):
        lo = slice(tile * LANES, (tile + 1) * LANES)
        hi = slice(half + tile * LANES, half + (tile + 1) * LANES)
        cos_y = jnp.where(step_y == 0.0, 1.0, table_ref[2:3, lo])
        sin_y = step_y * table_ref[3:4, lo]
        cosine = cos_x * cos_y - sin_x * sin_y
        sine = sin_x * cos_y + cos_x * sin_y
        real = part_ref[:, lo].astype(jnp.float32)
        imag = part_ref[:, hi].astype(jnp.float32)
        shifted[:, lo] = (real * cosine + imag * sine).astype(jnp.bfloat16)
        shifted[:, hi] = (imag * cosine - real * sine).astype(jnp.bfloat16)

    pl.semaphore_wait(barrier, n_ptl - 1 + n_lib - 1)

    def part(i, source, r):
        return gath.at[i, source, pl.ds((r % pieces) * piece_rows, piece_rows)]

    def z_copy(r):
        to = lax.rem(ptl + hop(r // pieces, n_ptl), n_ptl)
        return pltpu.make_async_remote_copy(
            src_ref=shifted.at[pl.ds((r % pieces) * piece_rows, piece_rows), chunk(to)],
            dst_ref=part(r // pieces, lib, r),
            send_sem=z_send.at[r - pieces],
            recv_sem=z_recv.at[r - pieces],
            device_id={"ptl": to},
        )

    for r in range(pieces, min(pieces + window, n_pieces)):
        z_copy(r).start()
    own_copy = pltpu.make_async_copy(shifted.at[:, chunk(ptl)], gath.at[0, lib], own_sem)
    own_copy.start()

    def x_source(d):
        return lax.rem(x - d + n_x, n_x) * 2 + core

    def lib_copy(r, d, source, send, recv, to):
        return pltpu.make_async_remote_copy(
            src_ref=part(r // pieces, source, r),
            dst_ref=part(r // pieces, source, r),
            send_sem=send.at[r, d],
            recv_sem=recv.at[r, d],
            device_id={"lib": to},
        )

    def x_copy(r, d):
        return lib_copy(r, d - 1, lib, x_send, x_recv, lax.rem(x + d, n_x) * 2 + core)

    def x_arrival(r, d):
        return lib_copy(r, d - 1, x_source(d), x_send, x_recv, x_source(d))

    def core_copy(r, d):
        return lib_copy(r, d, x_source(d), c_send, c_recv, mate)

    def core_arrival(r, d):
        return lib_copy(r, d, x_source(d) + 1 - 2 * core, c_send, c_recv, mate)

    def z_arrival(r):
        return pltpu.make_async_remote_copy(
            src_ref=part(r // pieces, lib, r),
            dst_ref=part(r // pieces, lib, r),
            send_sem=z_send.at[r - pieces],
            recv_sem=z_recv.at[r - pieces],
            device_id={"ptl": lax.rem(ptl - hop(r // pieces, n_ptl) + n_ptl, n_ptl)},
        )

    def spread(r):
        run_loop(1, n_x, lambda d: x_copy(r, d).start())
        core_copy(r, 0).start()

    def score_copy(i):
        return pltpu.make_async_remote_copy(
            src_ref=spart.at[i],
            dst_ref=srecv.at[i - 1],
            send_sem=s_send.at[i - 1],
            recv_sem=s_recv.at[i - 1],
            device_id={"ptl": lax.rem(ptl - hop(i, n_ptl) + n_ptl, n_ptl)},
        )

    def relay(r):
        def forward(d):
            x_arrival(r, d).wait_recv()
            core_copy(r, d).start()

        run_loop(1, n_x, forward)

    def score(i):
        for p in range(pieces):
            run_loop(0, n_x, lambda d: core_arrival(i * pieces + p, d).wait_recv())
        block = gath[i].reshape(n_lib * rows, span)
        spart[i] = (
            lax.dot_general(
                block, weighted[...], (((1,), (1,)), ((), ())), preferred_element_type=jnp.float32
            )
            - half_norm
        )

    own_copy.wait()
    for r in range(pieces):
        spread(r)

    noise2[:, 0:half] = noise_ref[...]
    noise2[:, half:width] = noise_ref[...]

    ref_copy.wait()
    offset = ptl * part_cols - first_tile(ptl) * LANES
    place = lax.broadcasted_iota(jnp.int32, (1, span), 1)
    inside = (place >= offset) & (place < offset + part_cols)
    noise = jnp.where(inside, noise2[:, chunk(ptl)], 0.0)
    widened = refbuf[...].astype(jnp.float32)
    scaled = widened * noise
    weighted[...] = scaled.astype(jnp.bfloat16)
    half_norm = to_row(0.5 * jnp.sum(widened * scaled, axis=1, keepdims=True))

    lag = min(2, pieces)
    for r in range(pieces - lag):
        relay(r)

    def group(i):
        for p in range(pieces):
            r = i * pieces + p
            z_arrival(r).wait_recv()
            spread(r)

            @pl.when(r + window < n_pieces)
            def _():
                z_copy(r + window).start()

            relay(r - lag)
        score(i - 1)

    group(1)

    def middle(i):
        group(i)
        score_copy(i - 1).start()

    run_loop(2, n_ptl, middle)
    for r in range(n_pieces - lag, n_pieces):
        relay(r)
    score(n_ptl - 1)
    score_copy(n_ptl - 1).start()

    def add_scores(i):
        score_copy(i).wait_recv()
        spart[0] = spart[0] + srecv[i - 1]

    run_loop(1, n_ptl, add_scores)
    scores = spart[0]

    own_peak = jnp.max(scores, axis=1, keepdims=True)
    peak = to_row(own_peak)
    stat[0:1] = peak
    stat[1:2] = to_row(jnp.sum(jnp.exp(scores - own_peak), axis=1, keepdims=True))

    def stat_copy(d):
        return pltpu.make_async_remote_copy(
            src_ref=stat,
            dst_ref=stat_in.at[d],
            send_sem=t_send.at[d - 1],
            recv_sem=t_recv.at[d - 1],
            device_id={"lib": lax.rem(lib + d, n_lib)},
        )

    run_loop(1, n_lib, lambda d: stat_copy(d).start())
    stat_in[0, 0:2] = stat[0:2]
    run_loop(1, n_lib, lambda d: stat_copy(d).wait_recv())
    top = peak
    for d in range(1, n_lib):
        top = jnp.maximum(top, stat_in[d, 0:1])
    total = jnp.zeros_like(top)
    for d in range(n_lib):
        total = total + stat_in[d, 1:2] * jnp.exp(stat_in[d, 0:1] - top)
    evidence = top + jnp.log(total)
    own_evidence = evidence[:, 0:rows]
    for l in range(1, n_lib):
        own_evidence = jnp.where(lib == l, evidence[:, l * rows : (l + 1) * rows], own_evidence)
    evid_ref[...] = own_evidence
    own_post = jnp.exp(scores - to_column(evidence)).astype(jnp.bfloat16)
    post[0] = own_post

    def post_copy(i):
        return pltpu.make_async_remote_copy(
            src_ref=post.at[0],
            dst_ref=post.at[i],
            send_sem=p_send.at[i - 1],
            recv_sem=p_recv.at[i - 1],
            device_id={"ptl": lax.rem(ptl + hop(i, n_ptl), n_ptl)},
        )

    run_loop(1, n_ptl, lambda i: post_copy(i).start())

    onehot = (
        class_ref[...] == lax.broadcasted_iota(jnp.int32, (CLASSES, class_ref.shape[1]), 0)
    ).astype(jnp.bfloat16)
    shares = lax.dot_general(
        onehot, own_post, (((1,), (1,)), ((), ())), preferred_element_type=jnp.float32
    )
    for l in range(n_lib):
        share_out[l] = shares[:, l * rows : (l + 1) * rows]

    def share_copy(d):
        to = lax.rem(lib + d, n_lib)
        return pltpu.make_async_remote_copy(
            src_ref=share_out.at[to],
            dst_ref=share_in.at[d - 1],
            send_sem=h_send.at[d - 1],
            recv_sem=h_recv.at[d - 1],
            device_id={"lib": to},
        )

    run_loop(1, n_lib, lambda d: share_copy(d).start())

    def weigh(weights, images):
        return lax.dot_general(
            weights, images, (((0,), (0,)), ((), ())), preferred_element_type=jnp.float32
        )

    block = 512 if span % 512 == 0 else LANES

    def own_sums(b):
        cols = pl.ds(pl.multiple_of(b * block, block), block)
        images = gath[0, :, :, cols].reshape(n_lib * rows, block)
        own_part[:, cols] = weigh(own_post, images)

    lax.fori_loop(0, span // block, lambda b, c: (own_sums(b), c)[1], 0)

    ones = jnp.ones((8, n_lib * rows), jnp.bfloat16)

    def totals(weights):
        return lax.dot_general(
            ones, weights, (((1,), (0,)), ((), ())), preferred_element_type=jnp.float32
        )

    totbuf[...] = totals(own_post)
    run_loop(1, n_ptl, lambda i: post_copy(i).wait_recv())

    def add_total(i):
        totbuf[...] += totals(post[i])

    run_loop(1, n_ptl, add_total)

    def other_sums(b):
        cols = pl.ds(pl.multiple_of(b * block, block), block)
        sums = own_part[:, cols]
        for i in range(1, n_ptl):
            images = gath[i, :, :, cols].reshape(n_lib * rows, block)
            sums = sums + weigh(post[i], images)
        sums_ref[cols, :] = sums.T

    lax.fori_loop(0, span // block, lambda b, c: (other_sums(b), c)[1], 0)

    count = total_ref.shape[1]
    own_total = totbuf[0:1, 0:count]
    for z in range(1, n_ptl):
        own_total = jnp.where(ptl == z, totbuf[0:1, z * count : (z + 1) * count], own_total)
    total_ref[...] = own_total

    share = share_out[lib]
    for d in range(1, n_lib):
        share_copy(d).wait_recv()
        share = share + share_in[d - 1]
    share_ref[...] = share

    def ptl_sent(i):
        score_copy(i).wait_send()
        post_copy(i).wait_send()

    def lib_sent(d):
        stat_copy(d).wait_send()
        share_copy(d).wait_send()

    def spread_sent(r):
        run_loop(1, n_x, lambda d: x_copy(r, d).wait_send())
        run_loop(0, n_x, lambda d: core_copy(r, d).wait_send())

    run_loop(1, n_ptl, ptl_sent)
    run_loop(1, n_lib, lib_sent)
    run_loop(pieces, n_pieces, lambda r: z_copy(r).wait_send())
    run_loop(0, n_pieces, spread_sent)


def finish(n_ptl, sums_in, evid_in, share_in, total_in, sums, evid, share, total, sem):
    part_cols = sums.shape[0]
    span = sums_in.shape[0]
    z = lax.axis_index("ptl")
    tiles = n_ptl * part_cols // LANES
    offset = z * part_cols - jnp.minimum((z * part_cols) // LANES, tiles - span // LANES) * LANES
    copy = pltpu.make_async_copy(
        sums_in.at[pl.ds(pl.multiple_of(offset, 8), part_cols)], sums, sem
    )
    copy.start()
    evid[...] = evid_in[...]
    share[...] = share_in[...]
    total[...] = total_in[...]
    copy.wait()


def trig_table(half):
    index = np.arange(half)
    angle_x = (index % 64) * (2.0 * math.pi / 128.0)
    angle_y = (index // 64) * (2.0 * math.pi / 128.0)
    table = np.zeros((8, half), np.float32)
    table[0], table[1] = np.cos(angle_x), np.sin(angle_x)
    table[2], table[3] = np.cos(angle_y), np.sin(angle_y)
    return table


def on_device(n_lib, n_ptl, particles, shifts, references, inv_noise, proj_class):
    rows, width = particles.shape
    projections = references.shape[0]
    part_cols = width // n_ptl
    tiles = width // LANES
    cover = max(-(-(z * part_cols % LANES + part_cols) // LANES) for z in range(n_ptl))
    span = min(cover, tiles) * LANES
    n_x = n_lib // 2
    group = n_lib * rows
    own_total = projections // n_ptl
    pieces = 3 if rows % 48 == 0 else 1
    window = WINDOW
    n_pieces = n_ptl * pieces
    vmem = pl.BlockSpec(memory_space=pltpu.VMEM)
    dma = pltpu.SemaphoreType.DMA
    sums, evidence, share, total = pl.pallas_call(
        functools.partial(kernel, n_lib, n_ptl, span, pieces, window),
        out_shape=(
            jax.ShapeDtypeStruct((span, projections), jnp.float32),
            jax.ShapeDtypeStruct((1, rows), jnp.float32),
            jax.ShapeDtypeStruct((CLASSES, rows), jnp.float32),
            jax.ShapeDtypeStruct((1, own_total), jnp.float32),
        ),
        in_specs=[vmem, vmem, vmem, pl.BlockSpec(memory_space=pl.ANY), vmem, vmem],
        out_specs=(vmem, vmem, vmem, vmem),
        scratch_shapes=[
            pltpu.VMEM((1, width), jnp.float32),
            pltpu.VMEM((rows, width), jnp.bfloat16),
            pltpu.VMEM((n_ptl, n_lib, rows, span), jnp.bfloat16),
            pltpu.VMEM((projections, span), jnp.bfloat16),
            pltpu.VMEM((projections, span), jnp.bfloat16),
            pltpu.VMEM((n_ptl, group, projections), jnp.float32),
            pltpu.VMEM((n_ptl - 1, group, projections), jnp.float32),
            pltpu.VMEM((n_ptl, group, projections), jnp.bfloat16),
            pltpu.VMEM((8, group), jnp.float32),
            pltpu.VMEM((n_lib, 8, group), jnp.float32),
            pltpu.VMEM((n_lib, CLASSES, rows), jnp.float32),
            pltpu.VMEM((n_lib - 1, CLASSES, rows), jnp.float32),
            pltpu.VMEM((8, projections), jnp.float32),
            pltpu.VMEM((projections, span), jnp.float32),
            dma,
            dma,
            dma((n_pieces - pieces,)),
            dma((n_pieces - pieces,)),
            dma((n_pieces, n_x - 1)),
            dma((n_pieces, n_x - 1)),
            dma((n_pieces, n_x)),
            dma((n_pieces, n_x)),
            dma((n_ptl - 1,)),
            dma((n_ptl - 1,)),
            dma((n_lib - 1,)),
            dma((n_lib - 1,)),
            dma((n_ptl - 1,)),
            dma((n_ptl - 1,)),
            dma((n_lib - 1,)),
            dma((n_lib - 1,)),
        ],
        compiler_params=pltpu.CompilerParams(
            collective_id=0, has_side_effects=True, vmem_limit_bytes=56 * 1024 * 1024
        ),
    )(
        particles,
        shifts[None, :],
        trig_table(width // 2),
        references,
        inv_noise[None, :],
        proj_class[None, :],
    )
    far = pl.BlockSpec(memory_space=pl.ANY)
    sums, evidence, share, total = pl.pallas_call(
        functools.partial(finish, n_ptl),
        out_shape=(
            jax.ShapeDtypeStruct((part_cols, projections), jnp.float32),
            jax.ShapeDtypeStruct((1, rows), jnp.float32),
            jax.ShapeDtypeStruct((CLASSES, rows), jnp.float32),
            jax.ShapeDtypeStruct((1, own_total), jnp.float32),
        ),
        in_specs=[vmem, vmem, vmem, vmem],
        out_specs=(far, vmem, vmem, vmem),
        scratch_shapes=[dma],
    )(sums, evidence, share, total)
    return evidence[0], share.T, sums.T, total[0]


def solution(mesh):
    in_specs = (
        P(("grp", "lib", "ptl"), None),
        P(("grp", "lib", "ptl")),
        P(("grp", "lib"), None),
        P("grp"),
        P("lib"),
    )
    out_specs = (
        P(("grp", "lib", "ptl")),
        P(("grp", "lib", "ptl"), None),
        P(("grp", "lib"), "ptl"),
        P(("grp", "lib", "ptl")),
    )
    return jax.shard_map(
        functools.partial(on_device, mesh.shape["lib"], mesh.shape["ptl"]),
        mesh=mesh,
        in_specs=in_specs,
        out_specs=out_specs,
        check_vma=False,
    )
```

```python
import functools
import math

import jax
import jax.numpy as jnp
import numpy as np
from jax import lax
from jax.experimental import pallas as pl
from jax.experimental.pallas import tpu as pltpu
from jax.sharding import PartitionSpec as P

CLASSES = 16
WINDOW = 4
LANES = 128


def run_loop(low, high, body):
    if high - low <= 4:
        for index in range(low, high):
            body(index)
    else:

        def step(index, carry):
            body(index)
            return carry

        lax.fori_loop(low, high, step, 0)


def hop(index, count):
    odd = index % 2
    return odd * ((index + 1) // 2) + (1 - odd) * (count - index // 2)


def diagonal(count):
    shape = (count, count)
    return lax.broadcasted_iota(jnp.int32, shape, 0) == lax.broadcasted_iota(jnp.int32, shape, 1)


def to_column(row):
    return jnp.sum(jnp.where(diagonal(row.shape[1]), row, 0.0), axis=1, keepdims=True)


def to_row(column):
    return jnp.sum(jnp.where(diagonal(column.shape[0]), column, 0.0), axis=0, keepdims=True)


def kernel(
    n_lib,
    n_ptl,
    span,
    pieces,
    window,
    part_hbm,
    shift_ref,
    table_ref,
    refs_hbm,
    noise_ref,
    class_ref,
    sums_ref,
    evid_ref,
    share_ref,
    total_ref,
    noise2,
    part_ref,
    shifted,
    gath,
    refbuf,
    weighted,
    spart,
    srecv,
    post,
    stat,
    stat_in,
    share_out,
    share_in,
    totbuf,
    own_part,
    part_sem,
    ref_sem,
    own_sem,
    z_send,
    z_recv,
    x_send,
    x_recv,
    c_send,
    c_recv,
    s_send,
    s_recv,
    t_send,
    t_recv,
    p_send,
    p_recv,
    h_send,
    h_recv,
):
    lib = lax.axis_index("lib")
    ptl = lax.axis_index("ptl")
    n_x = n_lib // 2
    x, core = lib // 2, lib % 2
    mate = 2 * x + 1 - core
    rows, width = part_ref.shape
    half = width // 2
    part_cols = width // n_ptl
    tiles = width // LANES
    piece_rows = rows // pieces
    n_pieces = n_ptl * pieces

    def first_tile(z):
        return jnp.minimum((z * part_cols) // LANES, tiles - span // LANES)

    def chunk(z):
        return pl.ds(pl.multiple_of(first_tile(z) * LANES, LANES), span)

    part_copy = pltpu.make_async_copy(part_hbm, part_ref, part_sem)
    part_copy.start()
    barrier = pltpu.get_barrier_semaphore()

    def greet_ptl(step):
        pl.semaphore_signal(barrier, inc=1, device_id={"ptl": lax.rem(ptl + step, n_ptl)})

    def greet_lib(step):
        pl.semaphore_signal(barrier, inc=1, device_id={"lib": lax.rem(lib + step, n_lib)})

    run_loop(1, n_ptl, greet_ptl)
    run_loop(1, n_lib, greet_lib)

    ref_copy = pltpu.make_async_copy(refs_hbm.at[:, chunk(ptl)], refbuf, ref_sem)
    ref_copy.start()

    ids = to_column(shift_ref[...].astype(jnp.float32)).astype(jnp.int32)
    step_y = (ids >= 3).astype(jnp.int32) + (ids >= 6).astype(jnp.int32)
    step_x = (ids - 3 * step_y - 1).astype(jnp.float32)
    step_y = (step_y - 1).astype(jnp.float32)
    cos_x = jnp.where(step_x == 0.0, 1.0, table_ref[0:1, 0:LANES])
    sin_x = step_x * table_ref[1:2, 0:LANES]
    part_copy.wait()
    for tile in range(half // LANES):
        lo = slice(tile * LANES, (tile + 1) * LANES)
        hi = slice(half + tile * LANES, half + (tile + 1) * LANES)
        cos_y = jnp.where(step_y == 0.0, 1.0, table_ref[2:3, lo])
        sin_y = step_y * table_ref[3:4, lo]
        cosine = cos_x * cos_y - sin_x * sin_y
        sine = sin_x * cos_y + cos_x * sin_y
        real = part_ref[:, lo].astype(jnp.float32)
        imag = part_ref[:, hi].astype(jnp.float32)
        shifted[:, lo] = (real * cosine + imag * sine).astype(jnp.bfloat16)
        shifted[:, hi] = (imag * cosine - real * sine).astype(jnp.bfloat16)

    pl.semaphore_wait(barrier, n_ptl - 1 + n_lib - 1)

    def part(i, source, r):
        return gath.at[i, source, pl.ds((r % pieces) * piece_rows, piece_rows)]

    def z_copy(r):
        to = lax.rem(ptl + hop(r // pieces, n_ptl), n_ptl)
        return pltpu.make_async_remote_copy(
            src_ref=shifted.at[pl.ds((r % pieces) * piece_rows, piece_rows), chunk(to)],
            dst_ref=part(r // pieces, lib, r),
            send_sem=z_send.at[r - pieces],
            recv_sem=z_recv.at[r - pieces],
            device_id={"ptl": to},
        )

    for r in range(pieces, min(pieces + window, n_pieces)):
        z_copy(r).start()
    own_copy = pltpu.make_async_copy(shifted.at[:, chunk(ptl)], gath.at[0, lib], own_sem)
    own_copy.start()

    def x_source(d):
        return lax.rem(x - d + n_x, n_x) * 2 + core

    def lib_copy(r, d, source, send, recv, to):
        return pltpu.make_async_remote_copy(
            src_ref=part(r // pieces, source, r),
            dst_ref=part(r // pieces, source, r),
            send_sem=send.at[r, d],
            recv_sem=recv.at[r, d],
            device_id={"lib": to},
        )

    def x_copy(r, d):
        return lib_copy(r, d - 1, lib, x_send, x_recv, lax.rem(x + d, n_x) * 2 + core)

    def x_arrival(r, d):
        return lib_copy(r, d - 1, x_source(d), x_send, x_recv, x_source(d))

    def core_copy(r, d):
        return lib_copy(r, d, x_source(d), c_send, c_recv, mate)

    def core_arrival(r, d):
        return lib_copy(r, d, x_source(d) + 1 - 2 * core, c_send, c_recv, mate)

    def z_arrival(r):
        return pltpu.make_async_remote_copy(
            src_ref=part(r // pieces, lib, r),
            dst_ref=part(r // pieces, lib, r),
            send_sem=z_send.at[r - pieces],
            recv_sem=z_recv.at[r - pieces],
            device_id={"ptl": lax.rem(ptl - hop(r // pieces, n_ptl) + n_ptl, n_ptl)},
        )

    def spread(r):
        run_loop(1, n_x, lambda d: x_copy(r, d).start())
        core_copy(r, 0).start()

    def score_copy(i):
        return pltpu.make_async_remote_copy(
            src_ref=spart.at[i],
            dst_ref=srecv.at[i - 1],
            send_sem=s_send.at[i - 1],
            recv_sem=s_recv.at[i - 1],
            device_id={"ptl": lax.rem(ptl - hop(i, n_ptl) + n_ptl, n_ptl)},
        )

    def relay(r):
        def forward(d):
            x_arrival(r, d).wait_recv()
            core_copy(r, d).start()

        run_loop(1, n_x, forward)

    def score(i):
        for p in range(pieces):
            run_loop(0, n_x, lambda d: core_arrival(i * pieces + p, d).wait_recv())
        block = gath[i].reshape(n_lib * rows, span)
        spart[i] = (
            lax.dot_general(
                block, weighted[...], (((1,), (1,)), ((), ())), preferred_element_type=jnp.float32
            )
            - half_norm
        )

    own_copy.wait()
    for r in range(pieces):
        spread(r)

    for tile in range(half // LANES):
        row = noise_ref[tile : tile + 1, :]
        noise2[:, tile * LANES : (tile + 1) * LANES] = row
        noise2[:, half + tile * LANES : half + (tile + 1) * LANES] = row

    ref_copy.wait()
    offset = ptl * part_cols - first_tile(ptl) * LANES
    place = lax.broadcasted_iota(jnp.int32, (1, span), 1)
    inside = (place >= offset) & (place < offset + part_cols)
    noise = jnp.where(inside, noise2[:, chunk(ptl)], 0.0)
    widened = refbuf[...].astype(jnp.float32)
    scaled = widened * noise
    weighted[...] = scaled.astype(jnp.bfloat16)
    half_norm = to_row(0.5 * jnp.sum(widened * scaled, axis=1, keepdims=True))

    lag = min(2, pieces)
    for r in range(pieces - lag):
        relay(r)

    def group(i):
        for p in range(pieces):
            r = i * pieces + p
            z_arrival(r).wait_recv()
            spread(r)

            @pl.when(r + window < n_pieces)
            def _():
                z_copy(r + window).start()

            relay(r - lag)
        score(i - 1)

    group(1)

    def middle(i):
        group(i)
        score_copy(i - 1).start()

    run_loop(2, n_ptl, middle)
    for r in range(n_pieces - lag, n_pieces):
        relay(r)
    score(n_ptl - 1)
    score_copy(n_ptl - 1).start()

    def add_scores(i):
        score_copy(i).wait_recv()
        spart[0] = spart[0] + srecv[i - 1]

    run_loop(1, n_ptl, add_scores)
    scores = spart[0]

    own_peak = jnp.max(scores, axis=1, keepdims=True)
    peak = to_row(own_peak)
    stat[0:1] = peak
    stat[1:2] = to_row(jnp.sum(jnp.exp(scores - own_peak), axis=1, keepdims=True))

    def stat_copy(d):
        return pltpu.make_async_remote_copy(
            src_ref=stat,
            dst_ref=stat_in.at[d],
            send_sem=t_send.at[d - 1],
            recv_sem=t_recv.at[d - 1],
            device_id={"lib": lax.rem(lib + d, n_lib)},
        )

    run_loop(1, n_lib, lambda d: stat_copy(d).start())
    stat_in[0, 0:2] = stat[0:2]
    run_loop(1, n_lib, lambda d: stat_copy(d).wait_recv())
    top = peak
    for d in range(1, n_lib):
        top = jnp.maximum(top, stat_in[d, 0:1])
    total = jnp.zeros_like(top)
    for d in range(n_lib):
        total = total + stat_in[d, 1:2] * jnp.exp(stat_in[d, 0:1] - top)
    evidence = top + jnp.log(total)
    own_evidence = evidence[:, 0:rows]
    for l in range(1, n_lib):
        own_evidence = jnp.where(lib == l, evidence[:, l * rows : (l + 1) * rows], own_evidence)
    evid_ref[...] = own_evidence
    own_post = jnp.exp(scores - to_column(evidence)).astype(jnp.bfloat16)
    post[0] = own_post

    def post_copy(i):
        return pltpu.make_async_remote_copy(
            src_ref=post.at[0],
            dst_ref=post.at[i],
            send_sem=p_send.at[i - 1],
            recv_sem=p_recv.at[i - 1],
            device_id={"ptl": lax.rem(ptl + hop(i, n_ptl), n_ptl)},
        )

    run_loop(1, n_ptl, lambda i: post_copy(i).start())

    onehot = (
        class_ref[...] == lax.broadcasted_iota(jnp.int32, (CLASSES, class_ref.shape[1]), 0)
    ).astype(jnp.bfloat16)
    shares = lax.dot_general(
        onehot, own_post, (((1,), (1,)), ((), ())), preferred_element_type=jnp.float32
    )
    for l in range(n_lib):
        share_out[l] = shares[:, l * rows : (l + 1) * rows]

    def share_copy(d):
        to = lax.rem(lib + d, n_lib)
        return pltpu.make_async_remote_copy(
            src_ref=share_out.at[to],
            dst_ref=share_in.at[d - 1],
            send_sem=h_send.at[d - 1],
            recv_sem=h_recv.at[d - 1],
            device_id={"lib": to},
        )

    run_loop(1, n_lib, lambda d: share_copy(d).start())

    def weigh(weights, images):
        return lax.dot_general(
            weights, images, (((0,), (0,)), ((), ())), preferred_element_type=jnp.float32
        )

    block = 512 if span % 512 == 0 else LANES

    def own_sums(b):
        cols = pl.ds(pl.multiple_of(b * block, block), block)
        images = gath[0, :, :, cols].reshape(n_lib * rows, block)
        own_part[:, cols] = weigh(own_post, images)

    lax.fori_loop(0, span // block, lambda b, c: (own_sums(b), c)[1], 0)

    ones = jnp.ones((8, n_lib * rows), jnp.bfloat16)

    def totals(weights):
        return lax.dot_general(
            ones, weights, (((1,), (0,)), ((), ())), preferred_element_type=jnp.float32
        )

    totbuf[...] = totals(own_post)
    run_loop(1, n_ptl, lambda i: post_copy(i).wait_recv())

    def add_total(i):
        totbuf[...] += totals(post[i])

    run_loop(1, n_ptl, add_total)

    def other_sums(b):
        cols = pl.ds(pl.multiple_of(b * block, block), block)
        sums = own_part[:, cols]
        for i in range(1, n_ptl):
            images = gath[i, :, :, cols].reshape(n_lib * rows, block)
            sums = sums + weigh(post[i], images)
        sums_ref[cols, :] = sums.T

    lax.fori_loop(0, span // block, lambda b, c: (other_sums(b), c)[1], 0)

    count = total_ref.shape[1]
    own_total = totbuf[0:1, 0:count]
    for z in range(1, n_ptl):
        own_total = jnp.where(ptl == z, totbuf[0:1, z * count : (z + 1) * count], own_total)
    total_ref[...] = own_total

    share = share_out[lib]
    for d in range(1, n_lib):
        share_copy(d).wait_recv()
        share = share + share_in[d - 1]
    share_ref[...] = share

    def ptl_sent(i):
        score_copy(i).wait_send()
        post_copy(i).wait_send()

    def lib_sent(d):
        stat_copy(d).wait_send()
        share_copy(d).wait_send()

    def spread_sent(r):
        run_loop(1, n_x, lambda d: x_copy(r, d).wait_send())
        run_loop(0, n_x, lambda d: core_copy(r, d).wait_send())

    run_loop(1, n_ptl, ptl_sent)
    run_loop(1, n_lib, lib_sent)
    run_loop(pieces, n_pieces, lambda r: z_copy(r).wait_send())
    run_loop(0, n_pieces, spread_sent)


def finish(
    n_ptl, sums_in, evid_in, share_in, total_in, sums, evid, share, total, buffer, read_sem, write_sem
):
    part_cols = sums.shape[0]
    span = sums_in.shape[0]
    z = lax.axis_index("ptl")
    tiles = n_ptl * part_cols // LANES
    offset = z * part_cols - jnp.minimum((z * part_cols) // LANES, tiles - span // LANES) * LANES
    chunks = buffer.shape[0]
    step = part_cols // chunks

    def read(c):
        rows = pl.ds(pl.multiple_of(offset + c * step, 8), step)
        return pltpu.make_async_copy(sums_in.at[rows], buffer.at[c], read_sem.at[c])

    def write(c):
        return pltpu.make_async_copy(
            buffer.at[c], sums.at[pl.ds(c * step, step)], write_sem.at[c]
        )

    for c in range(chunks):
        read(c).start()
    evid[...] = evid_in[...]
    share[...] = share_in[...]
    total[...] = total_in[...]
    for c in range(chunks):
        read(c).wait()
        write(c).start()
    for c in range(chunks):
        write(c).wait()


def trig_table(half):
    index = np.arange(half)
    angle_x = (index % 64) * (2.0 * math.pi / 128.0)
    angle_y = (index // 64) * (2.0 * math.pi / 128.0)
    table = np.zeros((8, half), np.float32)
    table[0], table[1] = np.cos(angle_x), np.sin(angle_x)
    table[2], table[3] = np.cos(angle_y), np.sin(angle_y)
    return table


def on_device(n_lib, n_ptl, particles, shifts, references, inv_noise, proj_class):
    rows, width = particles.shape
    projections = references.shape[0]
    part_cols = width // n_ptl
    tiles = width // LANES
    cover = max(-(-(z * part_cols % LANES + part_cols) // LANES) for z in range(n_ptl))
    span = min(cover, tiles) * LANES
    n_x = n_lib // 2
    group = n_lib * rows
    own_total = projections // n_ptl
    pieces = 3 if rows % 48 == 0 else 1
    window = WINDOW
    n_pieces = n_ptl * pieces
    vmem = pl.BlockSpec(memory_space=pltpu.VMEM)
    far = pl.BlockSpec(memory_space=pl.ANY)
    dma = pltpu.SemaphoreType.DMA
    sums, evidence, share, total = pl.pallas_call(
        functools.partial(kernel, n_lib, n_ptl, span, pieces, window),
        out_shape=(
            jax.ShapeDtypeStruct((span, projections), jnp.float32),
            jax.ShapeDtypeStruct((1, rows), jnp.float32),
            jax.ShapeDtypeStruct((CLASSES, rows), jnp.float32),
            jax.ShapeDtypeStruct((1, own_total), jnp.float32),
        ),
        in_specs=[far, vmem, vmem, far, vmem, vmem],
        out_specs=(vmem, vmem, vmem, vmem),
        scratch_shapes=[
            pltpu.VMEM((1, width), jnp.float32),
            pltpu.VMEM((rows, width), jnp.bfloat16),
            pltpu.VMEM((rows, width), jnp.bfloat16),
            pltpu.VMEM((n_ptl, n_lib, rows, span), jnp.bfloat16),
            pltpu.VMEM((projections, span), jnp.bfloat16),
            pltpu.VMEM((projections, span), jnp.bfloat16),
            pltpu.VMEM((n_ptl, group, projections), jnp.float32),
            pltpu.VMEM((n_ptl - 1, group, projections), jnp.float32),
            pltpu.VMEM((n_ptl, group, projections), jnp.bfloat16),
            pltpu.VMEM((8, group), jnp.float32),
            pltpu.VMEM((n_lib, 8, group), jnp.float32),
            pltpu.VMEM((n_lib, CLASSES, rows), jnp.float32),
            pltpu.VMEM((n_lib - 1, CLASSES, rows), jnp.float32),
            pltpu.VMEM((8, projections), jnp.float32),
            pltpu.VMEM((projections, span), jnp.float32),
            dma,
            dma,
            dma,
            dma((n_pieces - pieces,)),
            dma((n_pieces - pieces,)),
            dma((n_pieces, n_x - 1)),
            dma((n_pieces, n_x - 1)),
            dma((n_pieces, n_x)),
            dma((n_pieces, n_x)),
            dma((n_ptl - 1,)),
            dma((n_ptl - 1,)),
            dma((n_lib - 1,)),
            dma((n_lib - 1,)),
            dma((n_ptl - 1,)),
            dma((n_ptl - 1,)),
            dma((n_lib - 1,)),
            dma((n_lib - 1,)),
        ],
        compiler_params=pltpu.CompilerParams(
            collective_id=0, has_side_effects=True, vmem_limit_bytes=56 * 1024 * 1024
        ),
    )(
        particles,
        shifts[None, :],
        trig_table(width // 2),
        references,
        inv_noise.reshape(-1, LANES),
        proj_class[None, :],
    )
    chunks = next(c for c in (6, 4, 3, 2, 1) if part_cols % (8 * c) == 0)
    sums, evidence, share, total = pl.pallas_call(
        functools.partial(finish, n_ptl),
        out_shape=(
            jax.ShapeDtypeStruct((part_cols, projections), jnp.float32),
            jax.ShapeDtypeStruct((1, rows), jnp.float32),
            jax.ShapeDtypeStruct((CLASSES, rows), jnp.float32),
            jax.ShapeDtypeStruct((1, own_total), jnp.float32),
        ),
        in_specs=[far, vmem, vmem, vmem],
        out_specs=(far, vmem, vmem, vmem),
        scratch_shapes=[
            pltpu.VMEM((chunks, part_cols // chunks, projections), jnp.float32),
            dma((chunks,)),
            dma((chunks,)),
        ],
    )(sums, evidence, share, total)
    return evidence[0], share.T, sums.T, total[0]


def solution(mesh):
    in_specs = (
        P(("grp", "lib", "ptl"), None),
        P(("grp", "lib", "ptl")),
        P(("grp", "lib"), None),
        P("grp"),
        P("lib"),
    )
    out_specs = (
        P(("grp", "lib", "ptl")),
        P(("grp", "lib", "ptl"), None),
        P(("grp", "lib"), "ptl"),
        P(("grp", "lib", "ptl")),
    )
    return jax.shard_map(
        functools.partial(on_device, mesh.shape["lib"], mesh.shape["ptl"]),
        mesh=mesh,
        in_specs=in_specs,
        out_specs=out_specs,
        check_vma=False,
    )
```

```python
import functools
import math

import jax
import jax.numpy as jnp
import numpy as np
from jax import lax
from jax.experimental import pallas as pl
from jax.experimental.pallas import tpu as pltpu
from jax.sharding import PartitionSpec as P

CLASSES = 16
WINDOW = 4
LANES = 128


def run_loop(low, high, body):
    if high - low <= 4:
        for index in range(low, high):
            body(index)
    else:

        def step(index, carry):
            body(index)
            return carry

        lax.fori_loop(low, high, step, 0)


def hop(index, count):
    odd = index % 2
    return odd * ((index + 1) // 2) + (1 - odd) * (count - index // 2)


def diagonal(count):
    shape = (count, count)
    return lax.broadcasted_iota(jnp.int32, shape, 0) == lax.broadcasted_iota(jnp.int32, shape, 1)


def to_column(row):
    return jnp.sum(jnp.where(diagonal(row.shape[1]), row, 0.0), axis=1, keepdims=True)


def to_row(column):
    return jnp.sum(jnp.where(diagonal(column.shape[0]), column, 0.0), axis=0, keepdims=True)


def kernel(
    n_lib,
    n_ptl,
    span,
    pieces,
    window,
    part_hbm,
    shift_ref,
    table_ref,
    refs_hbm,
    noise_ref,
    class_ref,
    sums_ref,
    evid_ref,
    share_ref,
    total_ref,
    noise2,
    part_ref,
    shifted,
    gath,
    refbuf,
    weighted,
    spart,
    srecv,
    post,
    stat,
    stat_in,
    share_out,
    share_in,
    totbuf,
    own_part,
    part_sem,
    ref_sem,
    own_sem,
    z_send,
    z_recv,
    x_send,
    x_recv,
    c_send,
    c_recv,
    s_send,
    s_recv,
    t_send,
    t_recv,
    p_send,
    p_recv,
    h_send,
    h_recv,
):
    lib = lax.axis_index("lib")
    ptl = lax.axis_index("ptl")
    n_x = n_lib // 2
    x, core = lib // 2, lib % 2
    mate = 2 * x + 1 - core
    rows, width = part_ref.shape
    half = width // 2
    part_cols = width // n_ptl
    tiles = width // LANES
    piece_rows = rows // pieces
    n_pieces = n_ptl * pieces

    def first_tile(z):
        return jnp.minimum((z * part_cols) // LANES, tiles - span // LANES)

    def chunk(z):
        return pl.ds(pl.multiple_of(first_tile(z) * LANES, LANES), span)

    part_copy = pltpu.make_async_copy(part_hbm, part_ref, part_sem)
    part_copy.start()
    barrier = pltpu.get_barrier_semaphore()

    def greet_ptl(step):
        pl.semaphore_signal(barrier, inc=1, device_id={"ptl": lax.rem(ptl + step, n_ptl)})

    def greet_lib(step):
        pl.semaphore_signal(barrier, inc=1, device_id={"lib": lax.rem(lib + step, n_lib)})

    run_loop(1, n_ptl, greet_ptl)
    run_loop(1, n_lib, greet_lib)

    ref_copy = pltpu.make_async_copy(refs_hbm.at[:, chunk(ptl)], refbuf, ref_sem)
    ref_copy.start()

    ids = to_column(shift_ref[...].astype(jnp.float32)).astype(jnp.int32)
    step_y = (ids >= 3).astype(jnp.int32) + (ids >= 6).astype(jnp.int32)
    step_x = (ids - 3 * step_y - 1).astype(jnp.float32)
    step_y = (step_y - 1).astype(jnp.float32)
    cos_x = jnp.where(step_x == 0.0, 1.0, table_ref[0:1, 0:LANES])
    sin_x = step_x * table_ref[1:2, 0:LANES]
    part_copy.wait()
    for tile in range(half // LANES):
        lo = slice(tile * LANES, (tile + 1) * LANES)
        hi = slice(half + tile * LANES, half + (tile + 1) * LANES)
        cos_y = jnp.where(step_y == 0.0, 1.0, table_ref[2:3, lo])
        sin_y = step_y * table_ref[3:4, lo]
        cosine = cos_x * cos_y - sin_x * sin_y
        sine = sin_x * cos_y + cos_x * sin_y
        real = part_ref[:, lo].astype(jnp.float32)
        imag = part_ref[:, hi].astype(jnp.float32)
        shifted[:, lo] = (real * cosine + imag * sine).astype(jnp.bfloat16)
        shifted[:, hi] = (imag * cosine - real * sine).astype(jnp.bfloat16)

    pl.semaphore_wait(barrier, n_ptl - 1 + n_lib - 1)

    def part(i, source, r):
        return gath.at[i, source, pl.ds((r % pieces) * piece_rows, piece_rows)]

    def z_copy(r):
        to = lax.rem(ptl + hop(r // pieces, n_ptl), n_ptl)
        return pltpu.make_async_remote_copy(
            src_ref=shifted.at[pl.ds((r % pieces) * piece_rows, piece_rows), chunk(to)],
            dst_ref=part(r // pieces, lib, r),
            send_sem=z_send.at[r - pieces],
            recv_sem=z_recv.at[r - pieces],
            device_id={"ptl": to},
        )

    for r in range(pieces, min(pieces + window, n_pieces)):
        z_copy(r).start()
    own_copy = pltpu.make_async_copy(shifted.at[:, chunk(ptl)], gath.at[0, lib], own_sem)
    own_copy.start()

    def x_source(d):
        return lax.rem(x - d + n_x, n_x) * 2 + core

    def lib_copy(r, d, source, send, recv, to):
        return pltpu.make_async_remote_copy(
            src_ref=part(r // pieces, source, r),
            dst_ref=part(r // pieces, source, r),
            send_sem=send.at[r, d],
            recv_sem=recv.at[r, d],
            device_id={"lib": to},
        )

    def x_copy(r, d):
        return lib_copy(r, d - 1, lib, x_send, x_recv, lax.rem(x + d, n_x) * 2 + core)

    def x_arrival(r, d):
        return lib_copy(r, d - 1, x_source(d), x_send, x_recv, x_source(d))

    def core_copy(r, d):
        return lib_copy(r, d, x_source(d), c_send, c_recv, mate)

    def core_arrival(r, d):
        return lib_copy(r, d, x_source(d) + 1 - 2 * core, c_send, c_recv, mate)

    def z_arrival(r):
        return pltpu.make_async_remote_copy(
            src_ref=part(r // pieces, lib, r),
            dst_ref=part(r // pieces, lib, r),
            send_sem=z_send.at[r - pieces],
            recv_sem=z_recv.at[r - pieces],
            device_id={"ptl": lax.rem(ptl - hop(r // pieces, n_ptl) + n_ptl, n_ptl)},
        )

    def spread(r):
        run_loop(1, n_x, lambda d: x_copy(r, d).start())
        core_copy(r, 0).start()

    def score_copy(i):
        return pltpu.make_async_remote_copy(
            src_ref=spart.at[i],
            dst_ref=srecv.at[i - 1],
            send_sem=s_send.at[i - 1],
            recv_sem=s_recv.at[i - 1],
            device_id={"ptl": lax.rem(ptl - hop(i, n_ptl) + n_ptl, n_ptl)},
        )

    def relay(r):
        def forward(d):
            x_arrival(r, d).wait_recv()
            core_copy(r, d).start()

        run_loop(1, n_x, forward)

    def score(i):
        for p in range(pieces):
            run_loop(0, n_x, lambda d: core_arrival(i * pieces + p, d).wait_recv())
        block = gath[i].reshape(n_lib * rows, span)
        spart[i] = (
            lax.dot_general(
                block, weighted[...], (((1,), (1,)), ((), ())), preferred_element_type=jnp.float32
            )
            - half_norm
        )

    own_copy.wait()
    for r in range(pieces):
        spread(r)

    for tile in range(half // LANES):
        row = noise_ref[tile : tile + 1, :]
        noise2[:, tile * LANES : (tile + 1) * LANES] = row
        noise2[:, half + tile * LANES : half + (tile + 1) * LANES] = row

    ref_copy.wait()
    offset = ptl * part_cols - first_tile(ptl) * LANES
    place = lax.broadcasted_iota(jnp.int32, (1, span), 1)
    inside = (place >= offset) & (place < offset + part_cols)
    noise = jnp.where(inside, noise2[:, chunk(ptl)], 0.0)
    widened = refbuf[...].astype(jnp.float32)
    scaled = widened * noise
    weighted[...] = scaled.astype(jnp.bfloat16)
    half_norm = to_row(0.5 * jnp.sum(widened * scaled, axis=1, keepdims=True))

    lag = min(2, pieces)
    for r in range(pieces - lag):
        relay(r)

    def group(i):
        for p in range(pieces):
            r = i * pieces + p
            z_arrival(r).wait_recv()
            spread(r)

            @pl.when(r + window < n_pieces)
            def _():
                z_copy(r + window).start()

            relay(r - lag)
        score(i - 1)

    group(1)

    def middle(i):
        group(i)
        score_copy(i - 1).start()

    run_loop(2, n_ptl, middle)
    for r in range(n_pieces - lag, n_pieces):
        relay(r)
    score(n_ptl - 1)
    score_copy(n_ptl - 1).start()

    def add_scores(i):
        score_copy(i).wait_recv()
        spart[0] = spart[0] + srecv[i - 1]

    run_loop(1, n_ptl, add_scores)
    scores = spart[0]

    own_peak = jnp.max(scores, axis=1, keepdims=True)
    peak = to_row(own_peak)
    stat[0:1] = peak
    stat[1:2] = to_row(jnp.sum(jnp.exp(scores - own_peak), axis=1, keepdims=True))

    def stat_copy(d):
        return pltpu.make_async_remote_copy(
            src_ref=stat,
            dst_ref=stat_in.at[d],
            send_sem=t_send.at[d - 1],
            recv_sem=t_recv.at[d - 1],
            device_id={"lib": lax.rem(lib + d, n_lib)},
        )

    run_loop(1, n_lib, lambda d: stat_copy(d).start())
    stat_in[0, 0:2] = stat[0:2]
    run_loop(1, n_lib, lambda d: stat_copy(d).wait_recv())
    top = peak
    for d in range(1, n_lib):
        top = jnp.maximum(top, stat_in[d, 0:1])
    total = jnp.zeros_like(top)
    for d in range(n_lib):
        total = total + stat_in[d, 1:2] * jnp.exp(stat_in[d, 0:1] - top)
    evidence = top + jnp.log(total)
    own_evidence = evidence[:, 0:rows]
    for l in range(1, n_lib):
        own_evidence = jnp.where(lib == l, evidence[:, l * rows : (l + 1) * rows], own_evidence)
    evid_ref[...] = own_evidence
    own_post = jnp.exp(scores - to_column(evidence)).astype(jnp.bfloat16)
    post[0] = own_post

    def post_copy(i):
        return pltpu.make_async_remote_copy(
            src_ref=post.at[0],
            dst_ref=post.at[i],
            send_sem=p_send.at[i - 1],
            recv_sem=p_recv.at[i - 1],
            device_id={"ptl": lax.rem(ptl + hop(i, n_ptl), n_ptl)},
        )

    run_loop(1, n_ptl, lambda i: post_copy(i).start())

    onehot = (
        class_ref[...] == lax.broadcasted_iota(jnp.int32, (CLASSES, class_ref.shape[1]), 0)
    ).astype(jnp.bfloat16)
    shares = lax.dot_general(
        onehot, own_post, (((1,), (1,)), ((), ())), preferred_element_type=jnp.float32
    )
    for l in range(n_lib):
        share_out[l] = shares[:, l * rows : (l + 1) * rows]

    def share_copy(d):
        to = lax.rem(lib + d, n_lib)
        return pltpu.make_async_remote_copy(
            src_ref=share_out.at[to],
            dst_ref=share_in.at[d - 1],
            send_sem=h_send.at[d - 1],
            recv_sem=h_recv.at[d - 1],
            device_id={"lib": to},
        )

    run_loop(1, n_lib, lambda d: share_copy(d).start())

    def weigh(weights, images):
        return lax.dot_general(
            weights, images, (((0,), (0,)), ((), ())), preferred_element_type=jnp.float32
        )

    block = 512 if span % 512 == 0 else LANES

    def own_sums(b):
        cols = pl.ds(pl.multiple_of(b * block, block), block)
        images = gath[0, :, :, cols].reshape(n_lib * rows, block)
        own_part[:, cols] = weigh(own_post, images)

    lax.fori_loop(0, span // block, lambda b, c: (own_sums(b), c)[1], 0)

    ones = jnp.ones((8, n_lib * rows), jnp.bfloat16)

    def totals(weights):
        return lax.dot_general(
            ones, weights, (((1,), (0,)), ((), ())), preferred_element_type=jnp.float32
        )

    totbuf[...] = totals(own_post)
    run_loop(1, n_ptl, lambda i: post_copy(i).wait_recv())

    def add_total(i):
        totbuf[...] += totals(post[i])

    run_loop(1, n_ptl, add_total)

    def other_sums(b):
        cols = pl.ds(pl.multiple_of(b * block, block), block)
        sums = own_part[:, cols]
        for i in range(1, n_ptl):
            images = gath[i, :, :, cols].reshape(n_lib * rows, block)
            sums = sums + weigh(post[i], images)
        sums_ref[cols, :] = sums.T

    lax.fori_loop(0, span // block, lambda b, c: (other_sums(b), c)[1], 0)

    count = total_ref.shape[1]
    own_total = totbuf[0:1, 0:count]
    for z in range(1, n_ptl):
        own_total = jnp.where(ptl == z, totbuf[0:1, z * count : (z + 1) * count], own_total)
    total_ref[...] = own_total

    share = share_out[lib]
    for d in range(1, n_lib):
        share_copy(d).wait_recv()
        share = share + share_in[d - 1]
    share_ref[...] = share

    def ptl_sent(i):
        score_copy(i).wait_send()
        post_copy(i).wait_send()

    def lib_sent(d):
        stat_copy(d).wait_send()
        share_copy(d).wait_send()

    def spread_sent(r):
        run_loop(1, n_x, lambda d: x_copy(r, d).wait_send())
        run_loop(0, n_x, lambda d: core_copy(r, d).wait_send())

    run_loop(1, n_ptl, ptl_sent)
    run_loop(1, n_lib, lib_sent)
    run_loop(pieces, n_pieces, lambda r: z_copy(r).wait_send())
    run_loop(0, n_pieces, spread_sent)


def finish(n_ptl, sums_in, evid_in, share_in, total_in, sums, evid, share, total, sem):
    part_cols = sums.shape[0]
    span = sums_in.shape[0]
    z = lax.axis_index("ptl")
    tiles = n_ptl * part_cols // LANES
    offset = z * part_cols - jnp.minimum((z * part_cols) // LANES, tiles - span // LANES) * LANES
    copy = pltpu.make_async_copy(
        sums_in.at[pl.ds(pl.multiple_of(offset, 8), part_cols)], sums, sem
    )
    copy.start()
    evid[...] = evid_in[...]
    share[...] = share_in[...]
    total[...] = total_in[...]
    copy.wait()


def trig_table(half):
    index = np.arange(half)
    angle_x = (index % 64) * (2.0 * math.pi / 128.0)
    angle_y = (index // 64) * (2.0 * math.pi / 128.0)
    table = np.zeros((8, half), np.float32)
    table[0], table[1] = np.cos(angle_x), np.sin(angle_x)
    table[2], table[3] = np.cos(angle_y), np.sin(angle_y)
    return table


def on_device(n_lib, n_ptl, particles, shifts, references, inv_noise, proj_class):
    rows, width = particles.shape
    projections = references.shape[0]
    part_cols = width // n_ptl
    tiles = width // LANES
    cover = max(-(-(z * part_cols % LANES + part_cols) // LANES) for z in range(n_ptl))
    span = min(cover, tiles) * LANES
    n_x = n_lib // 2
    group = n_lib * rows
    own_total = projections // n_ptl
    pieces = 3 if rows % 48 == 0 else 1
    window = WINDOW
    n_pieces = n_ptl * pieces
    vmem = pl.BlockSpec(memory_space=pltpu.VMEM)
    far = pl.BlockSpec(memory_space=pl.ANY)
    dma = pltpu.SemaphoreType.DMA
    sums, evidence, share, total = pl.pallas_call(
        functools.partial(kernel, n_lib, n_ptl, span, pieces, window),
        out_shape=(
            jax.ShapeDtypeStruct((span, projections), jnp.float32),
            jax.ShapeDtypeStruct((1, rows), jnp.float32),
            jax.ShapeDtypeStruct((CLASSES, rows), jnp.float32),
            jax.ShapeDtypeStruct((1, own_total), jnp.float32),
        ),
        in_specs=[far, vmem, vmem, far, vmem, vmem],
        out_specs=(vmem, vmem, vmem, vmem),
        scratch_shapes=[
            pltpu.VMEM((1, width), jnp.float32),
            pltpu.VMEM((rows, width), jnp.bfloat16),
            pltpu.VMEM((rows, width), jnp.bfloat16),
            pltpu.VMEM((n_ptl, n_lib, rows, span), jnp.bfloat16),
            pltpu.VMEM((projections, span), jnp.bfloat16),
            pltpu.VMEM((projections, span), jnp.bfloat16),
            pltpu.VMEM((n_ptl, group, projections), jnp.float32),
            pltpu.VMEM((n_ptl - 1, group, projections), jnp.float32),
            pltpu.VMEM((n_ptl, group, projections), jnp.bfloat16),
            pltpu.VMEM((8, group), jnp.float32),
            pltpu.VMEM((n_lib, 8, group), jnp.float32),
            pltpu.VMEM((n_lib, CLASSES, rows), jnp.float32),
            pltpu.VMEM((n_lib - 1, CLASSES, rows), jnp.float32),
            pltpu.VMEM((8, projections), jnp.float32),
            pltpu.VMEM((projections, span), jnp.float32),
            dma,
            dma,
            dma,
            dma((n_pieces - pieces,)),
            dma((n_pieces - pieces,)),
            dma((n_pieces, n_x - 1)),
            dma((n_pieces, n_x - 1)),
            dma((n_pieces, n_x)),
            dma((n_pieces, n_x)),
            dma((n_ptl - 1,)),
            dma((n_ptl - 1,)),
            dma((n_lib - 1,)),
            dma((n_lib - 1,)),
            dma((n_ptl - 1,)),
            dma((n_ptl - 1,)),
            dma((n_lib - 1,)),
            dma((n_lib - 1,)),
        ],
        compiler_params=pltpu.CompilerParams(
            collective_id=0, has_side_effects=True, vmem_limit_bytes=56 * 1024 * 1024
        ),
    )(
        particles,
        shifts[None, :],
        trig_table(width // 2),
        references,
        inv_noise.reshape(-1, LANES),
        proj_class[None, :],
    )
    sums, evidence, share, total = pl.pallas_call(
        functools.partial(finish, n_ptl),
        out_shape=(
            jax.ShapeDtypeStruct((part_cols, projections), jnp.float32),
            jax.ShapeDtypeStruct((1, rows), jnp.float32),
            jax.ShapeDtypeStruct((CLASSES, rows), jnp.float32),
            jax.ShapeDtypeStruct((1, own_total), jnp.float32),
        ),
        in_specs=[vmem, vmem, vmem, vmem],
        out_specs=(far, vmem, vmem, vmem),
        scratch_shapes=[dma],
    )(sums, evidence, share, total)
    return evidence[0], share.T, sums.T, total[0]


def solution(mesh):
    in_specs = (
        P(("grp", "lib", "ptl"), None),
        P(("grp", "lib", "ptl")),
        P(("grp", "lib"), None),
        P("grp"),
        P("lib"),
    )
    out_specs = (
        P(("grp", "lib", "ptl")),
        P(("grp", "lib", "ptl"), None),
        P(("grp", "lib"), "ptl"),
        P(("grp", "lib", "ptl")),
    )
    return jax.shard_map(
        functools.partial(on_device, mesh.shape["lib"], mesh.shape["ptl"]),
        mesh=mesh,
        in_specs=in_specs,
        out_specs=out_specs,
        check_vma=False,
    )
```
